256 devices in a mesh: row: 16 (over x_lo, y, core), col: 16 (over x_hi, z).
Axes of the slice: x: 4 (x_hi: 2, x_lo: 2; x = x_hi * 2 + x_lo), y: 4, z: 8, core: 2. Of those that a mesh axis runs over, the one named last changes fastest.
Arguments:
- slab: float32 [32768, 8192], P('row', 'col'), may hold values from -250 to 250
- sketch_op: float32 [256, 32768], P(None, 'row'), may hold values from -0.03125 to 0.03125
- block_order: int32 [64], replicated, may hold values from 0 to 63, as said below
- pivots: int32 [2, 128], replicated, may hold values from 0 to 8191, as said below
Outputs:
- slab_out: float32 [32768, 8192], P('row', 'col')
- factor_rows: float32 [256, 8192], P(None, 'col')
- sketch_out: float32 [256, 8192], P(None, 'col')
The draws below stay inside these ranges and needn't reach their ends.
Inputs may be any that keep to these rules, and one draw needn't show every extreme that they name: A permutation of the 64 storage blocks; panel k uses block block_order[k]. `pivots`: each row holds 128 different storage columns, none of them in the storage blocks block_order[0 .. 1].
All inputs are finite; a program needn't handle non-finite values.
Results may differ from the reference program's by a relative error of at most 0.00012.
Values sent between devices are 32-bit elements; how exact they have to be, the bound alone decides.
No kernel may reach another device: no remote copies, remote signals or barrier semaphores. Data moves between devices by JAX's collectives and lax.ppermute only.
A program may use at most 64 MiB of HBM per device.

```python
import math
import jax
import jax.numpy as jnp
from jax import lax

NC = 8192
PW = 128
SK = 256
PANELS = 2
ROWS = 32768


def layout_draw(key):
    block_perm = jax.random.permutation(jax.random.fold_in(key, 11), NC // PW).astype(jnp.int32)
    columns = jnp.arange(NC, dtype=jnp.int32)
    block_ids = columns // PW
    excluded = jnp.any(block_ids[:, None] == block_perm[None, :PANELS], axis=1)
    chosen = []
    for panel_number in range(PANELS):
        jitter = jax.random.randint(jax.random.fold_in(key, 20 + panel_number), (NC,), 0, 1024).astype(jnp.int32)
        scores = jnp.where(excluded, -1 - columns, jitter * NC + columns)
        picked = lax.top_k(scores, PW)[1]
        chosen.append(picked.astype(jnp.int32))
    return (block_perm, jnp.stack(chosen))


def draw_block_order(key, part):
    return layout_draw(key)[0]


def draw_pivots(key, part):
    return layout_draw(key)[1]


def draw_slab(key, part):
    subkeys = jax.random.split(jax.random.fold_in(key, 5), 3)
    row_ramp = jnp.arange(ROWS, dtype=jnp.float32) / max(ROWS - 1, 1)
    row_scale = jnp.exp(jax.random.uniform(subkeys[0], (ROWS,), jnp.float32, math.log(0.3), math.log(3.0))) * 3.0 ** row_ramp
    col_scale = jnp.exp(jax.random.uniform(subkeys[1], (NC,), jnp.float32, math.log(0.3), math.log(3.0)))
    base = jnp.clip(jax.random.normal(subkeys[2], (ROWS, NC), jnp.float32), -6.0, 6.0)
    return base * row_scale[:, None] * col_scale[None, :]


def block_scale(own_key, shape, cuts, low, largest):
    factor_of, own = 1.0, jax.random.fold_in(own_key, 6)
    for dim, parts in cuts:
        steps = jnp.exp(jax.random.uniform(jax.random.fold_in(own, dim), (parts,), jnp.float32, low / len(cuts), largest / len(cuts)))
        factor_of = factor_of * jnp.repeat(steps, shape[dim] // parts).reshape([-1 if axis == dim else 1 for axis in range(len(shape))])
    return factor_of


def noise(stream_key, dims, width, limit, cuts=(), held_as=jnp.bfloat16):
    gain = block_scale(stream_key, dims, cuts, -0.22, 0.18) if cuts else 1.0
    values = jax.random.normal(stream_key, dims, jnp.float32) * width * gain
    return jnp.minimum(jnp.maximum(values, -limit), limit).astype(held_as)


def setup_inputs(seed: int = 0) -> dict:
    splits = jax.random.split(jax.random.key(seed), 5)
    slab = draw_slab(jax.random.fold_in(splits[4], 71), 0)
    sketch_op = noise(splits[1], (SK, ROWS), ROWS ** -0.5, 0.03125, ((1, 16),), jnp.float32)
    block_order = draw_block_order(jax.random.fold_in(splits[4], 71), 0)
    pivots = draw_pivots(jax.random.fold_in(splits[4], 71), 0)
    return dict(slab=slab, sketch_op=sketch_op, block_order=block_order, pivots=pivots)


def left_solve(lower_factor, values):
    return lax.linalg.triangular_solve(lower_factor, values, left_side=True, lower=True)

def right_solve(lower_factor, values):
    return lax.linalg.triangular_solve(lower_factor, values, left_side=False, lower=True, transpose_a=True)

def reference(slab, sketch_op, block_order, pivots):
    highest = lax.Precision.HIGHEST
    sketch = jnp.dot(sketch_op.astype(jnp.float32), slab.astype(jnp.float32), precision=highest, preferred_element_type=jnp.float32)
    columns = jnp.arange(NC, dtype=jnp.int32)
    finished = jnp.zeros((NC,), dtype=bool)
    factor_parts = []
    for panel_number in range(PANELS):
        block_start = (block_order[panel_number] * PW).astype(jnp.int32)
        pivot_list = pivots[panel_number]
        panel_cols = slab[:, pivot_list]
        displaced = lax.dynamic_slice_in_dim(slab, block_start, PW, 1)
        panel_sketch = sketch[:, pivot_list]
        displaced_sketch = lax.dynamic_slice_in_dim(sketch, block_start, PW, 1)
        slab = slab.at[:, pivot_list].set(displaced)
        slab = lax.dynamic_update_slice_in_dim(slab, panel_cols, block_start, 1)
        sketch = sketch.at[:, pivot_list].set(displaced_sketch)
        sketch = lax.dynamic_update_slice_in_dim(sketch, panel_sketch, block_start, 1)
        gram_matrix = jnp.dot(panel_cols.T.astype(jnp.float32), panel_cols.astype(jnp.float32), precision=highest, preferred_element_type=jnp.float32)
        lower_factor = jnp.linalg.cholesky(gram_matrix)
        ortho_basis = right_solve(lower_factor, panel_cols)
        projected = jnp.dot(ortho_basis.T.astype(jnp.float32), slab.astype(jnp.float32), precision=highest, preferred_element_type=jnp.float32)
        in_block = columns // PW == block_order[panel_number]
        factor_parts.append(jnp.where(finished[None, :], 0.0, projected))
        finished = finished | in_block
        update = jnp.dot(ortho_basis.astype(jnp.float32), projected.astype(jnp.float32), precision=highest, preferred_element_type=jnp.float32)
        slab = jnp.where(finished[None, :], slab, slab - update)
        sketch_basis = right_solve(lower_factor, panel_sketch)
        sketch_update = jnp.dot(sketch_basis.astype(jnp.float32), projected.astype(jnp.float32), precision=highest, preferred_element_type=jnp.float32)
        sketch = jnp.where(finished[None, :], 0.0, sketch - sketch_update)
    return (slab, jnp.concatenate(factor_parts, axis=0), sketch)
```

```python
import jax
import jax.numpy as jnp
from jax import lax
from jax.sharding import PartitionSpec as P

HI = lax.Precision.HIGHEST
F32 = jnp.float32

NX, NY, NCORE, NXH, NZ = 2, 4, 2, 2, 8
PAIR_CAP = 56
DEST_CAP = 32


def dot(a, b, ca, cb, precision=HI):
    return lax.dot_general(
        a, b, (((ca,), (cb,)), ((), ())), precision=precision, preferred_element_type=F32
    )


def row_perm(f):
    out = []
    for x in range(NX):
        for y in range(NY):
            for c in range(NCORE):
                u, v, w = f(x, y, c)
                out.append(((x * NY + y) * NCORE + c, (u * NY + v % NY) * NCORE + w))
    return out


def col_perm(f):
    out = []
    for x in range(NXH):
        for z in range(NZ):
            u, v = f(x, z)
            out.append((x * NZ + z, u * NZ + v % NZ))
    return out


Y_UP = row_perm(lambda x, y, c: (x, y + 1, c))
Y_DOWN = row_perm(lambda x, y, c: (x, y - 1, c))
X_SWAP = row_perm(lambda x, y, c: (1 - x, y, c))
CORE_SWAP = row_perm(lambda x, y, c: (x, y, 1 - c))
Z_UP = col_perm(lambda x, z: (x, z + 1))
Z_DOWN = col_perm(lambda x, z: (x, z - 1))
XH_SWAP = col_perm(lambda x, z: (1 - x, z))


def row(x, perm):
    return lax.ppermute(x, "row", perm)


def col(x, perm):
    return lax.ppermute(x, "col", perm)


def exchange_sum(x, axis):
    n = lax.axis_size(axis)
    parts = x.reshape(n, x.shape[0] // n, *x.shape[1:])
    return jnp.sum(lax.all_to_all(parts, axis, 0, 0), axis=0)


def all_sum(x, axis):
    n = lax.axis_size(axis)
    mine = exchange_sum(x, axis)
    spread = jnp.broadcast_to(mine[None], (n, *mine.shape))
    return lax.all_to_all(spread, axis, 0, 0).reshape(x.shape)


def gather_rows(x, place):
    m, w = x.shape
    half = m // 2
    up, down = row(x, Y_UP), row(x, Y_DOWN)
    far_top, far_low = row(up[:half], Y_UP), row(down[half:], Y_DOWN)
    y = (place // NCORE) % NY
    ring = jnp.stack([x, down, jnp.concatenate([far_top, far_low]), up])
    ring = jnp.concatenate([ring, ring])
    ring = lax.dynamic_slice_in_dim(ring, (NY - y) % NY, NY, 0)
    core = place % NCORE
    other = row(ring, CORE_SWAP)
    pair = jnp.stack(
        [jnp.where(core == 0, ring, other), jnp.where(core == 0, other, ring)], axis=1
    )
    far = row(pair, X_SWAP)
    xlo = place // (NCORE * NY)
    both = jnp.stack([jnp.where(xlo == 0, pair, far), jnp.where(xlo == 0, far, pair)])
    return both.reshape(16 * m, w)


def right_solve(lower_factor, values):
    return lax.linalg.triangular_solve(
        lower_factor, values, left_side=False, lower=True, transpose_a=True
    )


def lower_inverse(lower_factor):
    eye = jnp.eye(lower_factor.shape[0], dtype=F32)
    return lax.linalg.triangular_solve(lower_factor, eye, left_side=True, lower=True)


def general(slab, sketch_op, block_order, pivots):
    width, pw = slab.shape[1], pivots.shape[1]
    place = lax.axis_index("col")
    base = place * width
    cols = base + jnp.arange(width, dtype=jnp.int32)
    sketch = all_sum(dot(sketch_op, slab, 1, 0), "row")

    def panel(k, carry):
        slab, sketch, finished, factors = carry
        start = block_order[k] * pw
        owner = start // width
        offset = start - owner * width
        owns = place == owner
        local = pivots[k] - base
        selector = (jnp.arange(width)[:, None] == local[None, :]).astype(F32)
        targeted = jnp.sum(selector, axis=1) > 0.5
        both = jnp.concatenate([slab, sketch])
        block = lax.dynamic_slice_in_dim(both, offset, pw, 1)
        moved = jnp.concatenate(
            [dot(both, selector, 1, 0), jnp.where(owns, block, 0.0)], axis=1
        )
        moved = all_sum(moved, "col")
        panel_cols, displaced = moved[:, :pw], moved[:, pw:]
        both = lax.dynamic_update_slice_in_dim(
            both, jnp.where(owns, panel_cols, block), offset, 1
        )
        both = jnp.where(targeted[None, :], dot(displaced, selector, 1, 1), both)
        slab, sketch = both[: slab.shape[0]], both[slab.shape[0] :]
        panel_slab, panel_sketch = panel_cols[: slab.shape[0]], panel_cols[slab.shape[0] :]
        gram = all_sum(dot(panel_slab, panel_slab, 0, 0), "row")
        lower = jnp.linalg.cholesky(gram)
        basis = right_solve(lower, panel_slab)
        projected = all_sum(dot(basis, slab, 0, 0), "row")
        factors = lax.dynamic_update_slice_in_dim(
            factors, jnp.where(finished[None, :], 0.0, projected), k * pw, 0
        )
        finished = finished | (cols // pw == block_order[k])
        slab = jnp.where(finished[None, :], slab, slab - dot(basis, projected, 1, 0))
        update = dot(right_solve(lower, panel_sketch), projected, 1, 0)
        sketch = jnp.where(finished[None, :], 0.0, sketch - update)
        return slab, sketch, finished, factors

    carry = (
        slab,
        sketch,
        jnp.zeros((width,), dtype=bool),
        jnp.zeros((pivots.shape[0] * pw, width), F32),
    )
    slab, sketch, _, factors = lax.fori_loop(0, pivots.shape[0], panel, carry)
    return slab, factors, sketch


def rank_in_group(group, valid):
    n = group.shape[0]
    same = (group[:, None] == group[None, :]) & valid[None, :]
    earlier = jnp.arange(n)[None, :] < jnp.arange(n)[:, None]
    return jnp.sum((same & earlier).astype(jnp.int32), axis=1)


def plan(block_order, pivots, width):
    pw = pivots.shape[1]
    first, second = pivots[0], pivots[1]
    block0 = block_order[0] * pw
    block1 = block_order[1] * pw
    index = jnp.arange(pw, dtype=jnp.int32)
    meet = first[:, None] == second[None, :]
    hit = jnp.any(meet, axis=0)
    moved = block0 + jnp.sum(jnp.where(meet, index[:, None], 0), axis=0)
    source = jnp.concatenate([first, jnp.where(hit, moved, second)])
    home = jnp.concatenate([block0 + index, block1 + index])
    goal = jnp.concatenate([first, second])
    goes = jnp.concatenate([~jnp.any(meet, axis=1), jnp.ones((pw,), dtype=bool)])
    pair = (source // width) % NZ
    pair_rank = rank_in_group(pair, jnp.ones_like(goes))
    dest = goal // width
    dest_rank = rank_in_group(dest, goes)
    fits = (jnp.max(pair_rank) < PAIR_CAP) & (
        jnp.max(jnp.where(goes, dest_rank, 0)) < DEST_CAP
    )
    return source, pair, pair_rank, home, goal, goes, dest, dest_rank, hit, fits


def joint(slab, sketch_op, block_order, pivots, planned):
    source, pair, pair_rank, home, goal, goes, dest, dest_rank, hit = planned
    rows, width = slab.shape
    pw = pivots.shape[1]
    np_ = 2 * pw
    ncol = NXH * NZ
    place_row, place = lax.axis_index("row"), lax.axis_index("col")
    z, xhi = place % NZ, place // NZ
    base = place * width
    here = jnp.arange(width, dtype=jnp.int32)
    cols = base + here

    slots = jnp.arange(PAIR_CAP, dtype=jnp.int32)
    mine = (source // width == place)[None, :] & (pair_rank[None, :] == slots[:, None])
    slot_col = jnp.sum(jnp.where(mine, source[None, :] - base + 1, 0), axis=1) - 1
    take = (slot_col[:, None] == here[None, :]).astype(F32)
    packed = dot(take, slab, 1, 1)
    shard = packed + col(packed, XH_SWAP)
    half = PAIR_CAP // 2 // 8 * 8
    up1, down1 = col(shard, Z_UP), col(shard, Z_DOWN)
    up2, down2 = col(up1, Z_UP), col(down1, Z_DOWN)
    up3, down3 = col(up2, Z_UP), col(down2, Z_DOWN)
    up4, down4 = col(up3[:half], Z_UP), col(down3[half:], Z_DOWN)

    sketch_part = exchange_sum(dot(sketch_op, slab, 1, 0), "row")

    taken = (home[:, None] == cols[None, :]) & goes[:, None]
    chunk = rows // ncol
    leaving = lax.dot_general(
        jnp.broadcast_to(taken.astype(F32)[None], (ncol, np_, width)),
        slab.reshape(ncol, chunk, width),
        (((2,), (2,)), ((0,), (0,))),
        precision=HI,
        preferred_element_type=F32,
    )
    leaving = leaving.reshape(NXH, NZ, np_, chunk)

    def for_z(step):
        return lax.dynamic_index_in_dim(leaving, (z + step) % NZ, 1, keepdims=False)

    stacked = jnp.concatenate(
        [shard, up1, up2, up3, up4, down4, down3, down2, down1], axis=0
    )
    relative = (z - pair) % NZ
    slot = relative * PAIR_CAP + pair_rank
    spread = (slot[:, None] == jnp.arange(NZ * PAIR_CAP)[None, :]).astype(F32)
    pivot_rows = dot(spread, stacked, 1, 0)

    gram_part = dot(pivot_rows, pivot_rows, 1, 1)
    sums = exchange_sum(
        jnp.concatenate(
            [gram_part, dot(sketch_op, pivot_rows, 1, 1), dot(pivot_rows, slab, 1, 0)],
            axis=1,
        ),
        "row",
    )
    gram = gather_rows(sums[:, :np_], place_row)

    far = for_z(4)
    first_cols = np_ // 2
    goes_up = col(far[:, :first_cols], Z_UP)
    goes_down = col(far[:, first_cols:], Z_DOWN)
    zero = jnp.zeros_like(goes_up)
    goes_up = for_z(3) + jnp.concatenate([goes_up, zero], axis=1)
    goes_down = for_z(-3) + jnp.concatenate([zero, goes_down], axis=1)
    for step in (2, 1):
        goes_up = for_z(step) + col(goes_up, Z_UP)
        goes_down = for_z(-step) + col(goes_down, Z_DOWN)
    arrived = for_z(0) + col(goes_up, Z_UP) + col(goes_down, Z_DOWN)
    keep = lax.dynamic_index_in_dim(arrived, xhi, 0, keepdims=False)
    give = lax.dynamic_index_in_dim(arrived, 1 - xhi, 0, keepdims=False)
    arrived = keep + col(give, XH_SWAP)
    by_goal = (
        ((dest * DEST_CAP + dest_rank)[None, :] == jnp.arange(ncol * DEST_CAP)[:, None])
        & goes[None, :]
    ).astype(F32)
    outgoing = dot(by_goal, arrived, 1, 0).reshape(ncol, DEST_CAP, chunk)
    pieces = jnp.concatenate([sums[:, np_ + sums.shape[0] * 16 :], sketch_part], axis=0)
    sent = dot(dot(by_goal, taken.astype(F32), 1, 0), pieces, 1, 1)
    sent = sent.reshape(ncol, DEST_CAP, pieces.shape[0])
    sent = jnp.pad(sent, ((0, 0), (0, 0), (0, chunk - pieces.shape[0])))
    outgoing = jnp.concatenate([outgoing, sent], axis=2)
    incoming = lax.all_to_all(outgoing, "col", 0, 0)
    new_rows = jnp.swapaxes(incoming[:, :, :chunk], 0, 1).reshape(DEST_CAP, rows)
    new_sums = jnp.sum(incoming[:, :, chunk : chunk + pieces.shape[0]], axis=0)

    wide = gather_rows(jnp.concatenate([sums[:, np_:], sketch_part], axis=1), place_row)
    pivot_sketch, product, sketch = (
        wide[:, :np_],
        wide[:, np_ : np_ + width],
        wide[:, np_ + width :],
    )
    small = pieces.shape[0] // 2
    late = gather_rows(
        jnp.concatenate([new_sums[:, :small].T, new_sums[:, small:].T], axis=1), place_row
    )
    new_product, new_sketch = late[:, :DEST_CAP], late[:, DEST_CAP:]

    lower0 = jnp.linalg.cholesky(gram[:pw, :pw])
    inv0 = lower_inverse(lower0)
    cross = dot(gram[pw:, :pw], inv0, 1, 1)
    lower1 = jnp.linalg.cholesky(gram[pw:, pw:] - dot(cross, cross, 1, 1))
    inv1 = lower_inverse(lower1)
    corner = -dot(inv1, dot(cross, inv0, 1, 0), 1, 0)
    inverse = jnp.concatenate(
        [
            jnp.concatenate([inv0, jnp.zeros_like(inv0)], axis=1),
            jnp.concatenate([corner, inv1], axis=1),
        ],
        axis=0,
    )

    in0 = cols // pw == block_order[0]
    in1 = cols // pw == block_order[1]
    at = (goal[:, None] == cols[None, :]) & goes[:, None]
    is_new = jnp.any(at, axis=0)
    slot_of = jnp.sum(jnp.where(at, dest_rank[:, None], 0), axis=0)
    put_new = (jnp.arange(DEST_CAP)[:, None] == slot_of[None, :]) & is_new[None, :]
    which = jnp.arange(np_, dtype=jnp.int32)
    put_pivot = (home[:, None] == cols[None, :])
    at0 = at & (which < pw)[:, None]
    is_new0 = jnp.any(at0, axis=0)
    put_new0 = put_new & is_new0[None, :]
    met = (pivots[1][:, None] == cols[None, :]) & hit[:, None]
    put_pivot0 = jnp.concatenate([put_pivot[:pw], met], axis=0)
    is_old0 = ~(is_new0 | in0 | jnp.any(met, axis=0))
    is_old = ~(is_new | in0 | in1)

    first_source = jnp.concatenate([new_product, gram], axis=1)
    put = jnp.concatenate([put_new, put_pivot], axis=0).astype(F32)
    put0 = jnp.concatenate([put_new0, put_pivot0], axis=0).astype(F32)
    before = jnp.where(is_old0[None, :], product, 0.0) + dot(first_source, put0, 1, 0)
    after = jnp.where(is_old[None, :], product, 0.0) + dot(first_source, put, 1, 0)
    top = dot(inverse[:pw], before, 1, 0)
    solved = dot(inverse, after, 1, 0)
    done = in0 | in1
    low = jnp.where(in0[None, :], 0.0, solved[pw:])
    factors = jnp.concatenate([top, low], axis=0)
    weights = jnp.concatenate(
        [
            jnp.where(in0[None, :], 0.0, solved[:pw]),
            jnp.where(done[None, :], 0.0, solved[pw:]),
        ],
        axis=0,
    )
    weights = dot(inverse, weights, 0, 0)
    mix = put - jnp.concatenate([jnp.zeros((DEST_CAP, width), F32), weights], axis=0)
    both_rows = jnp.concatenate([new_rows, pivot_rows], axis=0)
    slab_out = jnp.where(is_old[None, :], slab, 0.0) + dot(both_rows, mix, 0, 0)
    both_sketch = jnp.concatenate([new_sketch, pivot_sketch], axis=1)
    sketch_out = jnp.where(is_old[None, :], sketch, 0.0) + dot(both_sketch, mix, 1, 0)
    sketch_out = jnp.where(done[None, :], 0.0, sketch_out)
    return slab_out, factors, sketch_out


def local(slab, sketch_op, block_order, pivots):
    *planned, fits = plan(block_order, pivots, slab.shape[1])
    return lax.cond(
        fits,
        lambda *a: joint(*a),
        lambda *a: general(*a[:-1]),
        slab,
        sketch_op,
        block_order,
        pivots,
        planned,
    )


def solution(mesh):
    return jax.shard_map(
        local,
        mesh=mesh,
        in_specs=(P("row", "col"), P(None, "row"), P(), P()),
        out_specs=(P("row", "col"), P(None, "col"), P(None, "col")),
        check_vma=False,
    )
```

```python
import jax
import jax.numpy as jnp
from jax import lax
from jax.experimental import pallas as pl
from jax.experimental.pallas import tpu as pltpu
from jax.sharding import PartitionSpec as P

HI = lax.Precision.HIGHEST
F32 = jnp.float32

NXH, NZ = 2, 8
PAIR_CAP = 56
DEST_CAP = 32


def dot(a, b, ca, cb, precision=HI):
    return lax.dot_general(
        a, b, (((ca,), (cb,)), ((), ())), precision=precision, preferred_element_type=F32
    )


BLOCK = 128
STRIP = 16
VM = pl.BlockSpec(memory_space=pltpu.VMEM)
BF16 = jnp.bfloat16


def split2(x):
    high = x.astype(BF16)
    return high, (x - high.astype(F32)).astype(BF16)


def split3(x):
    high, rest = x.astype(BF16), None
    left = x - high.astype(F32)
    middle = left.astype(BF16)
    rest = (left - middle.astype(F32)).astype(BF16)
    return high, middle, rest


def dot3(a, b, ca, cb):
    a0, a1 = a
    b0, b1 = b
    return (
        dot(a0, b1, ca, cb, None) + dot(a1, b0, ca, cb, None)
    ) + dot(a0, b0, ca, cb, None)


def factor_block(s_ref, w_ref, n):
    sub = lax.broadcasted_iota(jnp.int32, (STRIP, n), 0)
    w_ref[...] = (
        lax.broadcasted_iota(jnp.int32, (n, n), 0) == lax.broadcasted_iota(jnp.int32, (n, n), 1)
    ).astype(F32)
    for start in range(0, n, STRIP):
        stop = start + STRIP
        v = s_ref[start:stop, :]
        w = w_ref[start:stop, :]
        lanes = [jnp.broadcast_to(v[:, start + m : start + m + 1], (STRIP, n)) for m in range(STRIP)]
        scale = jnp.zeros((STRIP, n), F32)
        for i in range(STRIP):
            pivot = lanes[i][i : i + 1, :]
            scale = jnp.where(sub == i, pivot, scale)
            if i == STRIP - 1:
                break
            f = jnp.where(sub > i, lanes[i] * (1.0 / pivot), 0.0)
            for m in range(i + 1, STRIP):
                lanes[m] = lanes[m] - f * lanes[m][i : i + 1, :]
            v = v - f * v[i : i + 1, :]
            w = w - f * w[i : i + 1, :]
        root = 1.0 / jnp.sqrt(scale)
        v, w = v * root, w * root
        w_ref[start:stop, :] = w
        if stop < n:
            update = dot(v, jnp.concatenate([v, w], axis=1), 0, 0)
            s_ref[stop:, :] = s_ref[stop:, :] - update[stop:, :n]
            w_ref[stop:, :] = w_ref[stop:, :] - update[stop:, n:]

def inverse_factor_kernel(gram_ref, out_ref, s_ref, w_ref):
    n = s_ref.shape[0]
    s_ref[...] = gram_ref[:n, :n]
    factor_block(s_ref, w_ref, n)
    inv0 = w_ref[...]
    if gram_ref.shape[0] == n:
        out_ref[...] = inv0
        return
    cross = dot(gram_ref[n:, :n], inv0, 1, 1)
    out_ref[:n, :n] = inv0
    out_ref[:n, n:] = jnp.zeros((n, n), F32)
    s_ref[...] = gram_ref[n:, n:] - dot(cross, cross, 1, 1)
    lead = dot(cross, inv0, 1, 0)
    factor_block(s_ref, w_ref, n)
    inv1 = w_ref[...]
    out_ref[n:, :n] = -dot(inv1, lead, 1, 0)
    out_ref[n:, n:] = inv1

def inverse_factor(gram):
    n = gram.shape[0]
    return pl.pallas_call(
        inverse_factor_kernel,
        out_shape=jax.ShapeDtypeStruct((n, n), F32),
        in_specs=[VM],
        out_specs=VM,
        scratch_shapes=[pltpu.VMEM((BLOCK, BLOCK), F32)] * 2,
        cost_estimate=pl.CostEstimate(flops=20_000_000, bytes_accessed=2 * n * n * 4, transcendentals=0),
        name="inverse_factor",
    )(gram)


def pack_kernel(slot_ref, slab_ref, out_ref):
    slots, width = out_ref.shape[0], slab_ref.shape[1]
    here = lax.broadcasted_iota(jnp.int32, (slots, width), 1)
    take = (slot_ref[...] == here).astype(F32).astype(BF16)
    step = 256
    for start in range(0, out_ref.shape[1], step):
        pieces = split3(slab_ref[start : start + step, :])
        out_ref[:, start : start + step] = sum(dot(take, p, 1, 1, None) for p in pieces[::-1])


def pack(slot_col, slab):
    slots, rows = slot_col.shape[0], slab.shape[0]
    return pl.pallas_call(
        pack_kernel,
        out_shape=jax.ShapeDtypeStruct((slots, rows), F32),
        in_specs=[VM, VM],
        out_specs=VM,
        cost_estimate=pl.CostEstimate(
            flops=6 * slots * slab.size, bytes_accessed=8 * slab.size, transcendentals=0
        ),
        name="pack",
    )(slot_col[:, None], slab)


def leave_kernel(where_ref, slab_ref, out_ref):
    chunks, _, chunk = out_ref.shape
    for k in range(2):
        rows = slice(k * BLOCK, (k + 1) * BLOCK)

        @pl.when(where_ref[2 * k] != 0)
        def _():
            offset = pl.multiple_of(where_ref[2 * k + 1], BLOCK)
            for m in range(chunks):
                part = slab_ref[m * chunk : (m + 1) * chunk, pl.ds(offset, BLOCK)]
                out_ref[m, rows, :] = part.T

        @pl.when(where_ref[2 * k] == 0)
        def _():
            out_ref[:, rows, :] = jnp.zeros((chunks, BLOCK, chunk), F32)


def leave(where, slab, chunks):
    rows = slab.shape[0]
    return pl.pallas_call(
        leave_kernel,
        out_shape=jax.ShapeDtypeStruct((chunks, 2 * BLOCK, rows // chunks), F32),
        in_specs=[pl.BlockSpec(memory_space=pltpu.SMEM), VM],
        out_specs=VM,
        cost_estimate=pl.CostEstimate(
            flops=slab.size, bytes_accessed=6 * slab.size, transcendentals=0
        ),
        name="leave",
    )(where, slab)


def project_kernel(slot_ref, slab_ref, op_ref, *refs):
    *shards, rows_ref, sums_ref, all_ref = refs
    count, total = slot_ref.shape[0], all_ref.shape[0]
    rows, width = slab_ref.shape
    start = 0
    for shard in shards:
        all_ref[start : start + shard.shape[0], :] = shard[...]
        start += shard.shape[0]
    spread = (
        slot_ref[...] == lax.broadcasted_iota(jnp.int32, (count, total), 1)
    ).astype(F32).astype(BF16)
    product = jnp.zeros((count, width), F32)
    sketch = jnp.zeros((op_ref.shape[0], count), F32)
    gram = jnp.zeros((count, count), F32)
    step = 512
    for at in range(0, rows, step):
        part = slice(at, at + step)
        pieces = split3(all_ref[:, part])
        pivot = sum(dot(spread, p, 1, 0, None) for p in pieces[::-1])
        rows_ref[:, part] = pivot
        two = split2(pivot)
        gram += dot(pivot, pivot, 1, 1)
        product += dot3(two, split2(slab_ref[part, :]), 1, 0)
        sketch += dot3(split2(op_ref[:, part]), two, 1, 1)
    sums_ref[:, :count] = gram
    sums_ref[:, count : 2 * count] = sketch
    sums_ref[:, 2 * count :] = product


def project(slot, slab, sketch_op, shards):
    count, (rows, width) = slot.shape[0], slab.shape
    total = sum(s.shape[0] for s in shards)
    shape = jax.ShapeDtypeStruct
    return pl.pallas_call(
        project_kernel,
        out_shape=(
            shape((count, rows), F32),
            shape((count, 2 * count + width), F32),
        ),
        in_specs=[VM] * (3 + len(shards)),
        out_specs=(VM, VM),
        scratch_shapes=[pltpu.VMEM((total, rows), F32)],
        cost_estimate=pl.CostEstimate(
            flops=6 * count * rows * (total + 2 * count + width),
            bytes_accessed=4 * (slab.size + sketch_op.size + total * rows + count * rows),
            transcendentals=0,
        ),
        name="project",
    )(slot[:, None], slab, sketch_op, *shards)


def sketch_kernel(op_ref, slab_ref, out_ref):
    acc = jnp.zeros(out_ref.shape, F32)
    for at in range(0, slab_ref.shape[0], 512):
        part = slice(at, at + 512)
        acc += dot3(split2(op_ref[:, part]), split2(slab_ref[part, :]), 1, 0)
    out_ref[...] = acc


def sketch_sum(sketch_op, slab):
    return pl.pallas_call(
        sketch_kernel,
        out_shape=jax.ShapeDtypeStruct((sketch_op.shape[0], slab.shape[1]), F32),
        in_specs=[VM, VM],
        out_specs=VM,
        cost_estimate=pl.CostEstimate(
            flops=6 * sketch_op.shape[0] * slab.size,
            bytes_accessed=4 * (slab.size + sketch_op.size),
            transcendentals=0,
        ),
        name="sketch_sum",
    )(sketch_op, slab)


def col_perm(f):
    out = []
    for x in range(NXH):
        for z in range(NZ):
            u, v = f(x, z)
            out.append((x * NZ + z, u * NZ + v % NZ))
    return out


Z_UP = col_perm(lambda x, z: (x, z + 1))
Z_DOWN = col_perm(lambda x, z: (x, z - 1))
XH_SWAP = col_perm(lambda x, z: (1 - x, z))


def col(x, perm):
    return lax.ppermute(x, "col", perm)


def exchange_sum(x, axis):
    n = lax.axis_size(axis)
    parts = x.reshape(n, x.shape[0] // n, *x.shape[1:])
    return jnp.sum(lax.all_to_all(parts, axis, 0, 0), axis=0)


def all_sum(x, axis):
    n = lax.axis_size(axis)
    mine = exchange_sum(x, axis)
    spread = jnp.broadcast_to(mine[None], (n, *mine.shape))
    return lax.all_to_all(spread, axis, 0, 0).reshape(x.shape)


def spread_rows(x):
    n = lax.axis_size("row")
    copies = jnp.broadcast_to(x[None], (n, *x.shape))
    return lax.all_to_all(copies, "row", 0, 0).reshape(n * x.shape[0], x.shape[1])


def general(slab, sketch_op, block_order, pivots):
    width, pw = slab.shape[1], pivots.shape[1]
    place = lax.axis_index("col")
    base = place * width
    cols = base + jnp.arange(width, dtype=jnp.int32)
    sketch = all_sum(dot(sketch_op, slab, 1, 0), "row")

    def panel(k, carry):
        slab, sketch, finished, factors = carry
        start = block_order[k] * pw
        owner = start // width
        offset = start - owner * width
        owns = place == owner
        local = pivots[k] - base
        selector = (jnp.arange(width)[:, None] == local[None, :]).astype(F32)
        targeted = jnp.sum(selector, axis=1) > 0.5
        both = jnp.concatenate([slab, sketch])
        block = lax.dynamic_slice_in_dim(both, offset, pw, 1)
        moved = jnp.concatenate(
            [dot(both, selector, 1, 0), jnp.where(owns, block, 0.0)], axis=1
        )
        moved = all_sum(moved, "col")
        panel_cols, displaced = moved[:, :pw], moved[:, pw:]
        both = lax.dynamic_update_slice_in_dim(
            both, jnp.where(owns, panel_cols, block), offset, 1
        )
        both = jnp.where(targeted[None, :], dot(displaced, selector, 1, 1), both)
        slab, sketch = both[: slab.shape[0]], both[slab.shape[0] :]
        panel_slab, panel_sketch = panel_cols[: slab.shape[0]], panel_cols[slab.shape[0] :]
        gram = all_sum(dot(panel_slab, panel_slab, 0, 0), "row")
        inverse = inverse_factor(gram)
        basis = dot(panel_slab, inverse, 1, 1)
        projected = all_sum(dot(basis, slab, 0, 0), "row")
        factors = lax.dynamic_update_slice_in_dim(
            factors, jnp.where(finished[None, :], 0.0, projected), k * pw, 0
        )
        finished = finished | (cols // pw == block_order[k])
        slab = jnp.where(finished[None, :], slab, slab - dot(basis, projected, 1, 0))
        update = dot(dot(panel_sketch, inverse, 1, 1), projected, 1, 0)
        sketch = jnp.where(finished[None, :], 0.0, sketch - update)
        return slab, sketch, finished, factors

    carry = (
        slab,
        sketch,
        jnp.zeros((width,), dtype=bool),
        jnp.zeros((pivots.shape[0] * pw, width), F32),
    )
    slab, sketch, _, factors = lax.fori_loop(0, pivots.shape[0], panel, carry)
    return slab, factors, sketch


def rank_in_group(group, valid):
    n = group.shape[0]
    same = (group[:, None] == group[None, :]) & valid[None, :]
    earlier = jnp.arange(n)[None, :] < jnp.arange(n)[:, None]
    return jnp.sum((same & earlier).astype(jnp.int32), axis=1)


def plan(block_order, pivots, width):
    pw = pivots.shape[1]
    first, second = pivots[0], pivots[1]
    block0 = block_order[0] * pw
    block1 = block_order[1] * pw
    index = jnp.arange(pw, dtype=jnp.int32)
    meet = first[:, None] == second[None, :]
    hit = jnp.any(meet, axis=0)
    moved = block0 + jnp.sum(jnp.where(meet, index[:, None], 0), axis=0)
    source = jnp.concatenate([first, jnp.where(hit, moved, second)])
    home = jnp.concatenate([block0 + index, block1 + index])
    goal = jnp.concatenate([first, second])
    goes = jnp.concatenate([~jnp.any(meet, axis=1), jnp.ones((pw,), dtype=bool)])
    pair = (source // width) % NZ
    pair_rank = rank_in_group(pair, jnp.ones_like(goes))
    dest = goal // width
    dest_rank = rank_in_group(dest, goes)
    fits = (jnp.max(pair_rank) < PAIR_CAP) & (
        jnp.max(jnp.where(goes, dest_rank, 0)) < DEST_CAP
    )
    return source, pair, pair_rank, home, goal, goes, dest, dest_rank, hit, fits


def joint(slab, sketch_op, block_order, pivots, planned):
    source, pair, pair_rank, home, goal, goes, dest, dest_rank, hit = planned
    rows, width = slab.shape
    pw = pivots.shape[1]
    np_ = 2 * pw
    ncol = NXH * NZ
    place_row, place = lax.axis_index("row"), lax.axis_index("col")
    z, xhi = place % NZ, place // NZ
    base = place * width
    here = jnp.arange(width, dtype=jnp.int32)
    cols = base + here

    slots = jnp.arange(PAIR_CAP, dtype=jnp.int32)
    mine = (source // width == place)[None, :] & (pair_rank[None, :] == slots[:, None])
    slot_col = jnp.sum(jnp.where(mine, source[None, :] - base + 1, 0), axis=1) - 1
    packed = pack(slot_col, slab)
    shard = packed + col(packed, XH_SWAP)
    half = PAIR_CAP // 2 // 8 * 8
    up1, down1 = col(shard, Z_UP), col(shard, Z_DOWN)
    up2, down2 = col(up1, Z_UP), col(down1, Z_DOWN)
    up3, down3 = col(up2, Z_UP), col(down2, Z_DOWN)
    up4, down4 = col(up3[:half], Z_UP), col(down3[half:], Z_DOWN)

    sketch_part = exchange_sum(sketch_sum(sketch_op, slab), "row")
    sketch = spread_rows(sketch_part)

    chunk = rows // ncol
    starts = block_order[:2] * pw
    owned = (starts // width == place).astype(jnp.int32)
    where = jnp.stack([owned, starts % width], axis=1).reshape(-1)
    leaving = leave(where, slab, ncol).reshape(NXH, NZ, np_, chunk)

    shards = (shard, up1, up2, up3, up4, down4, down3, down2, down1)
    slot = ((z - pair) % NZ) * PAIR_CAP + pair_rank
    leaving, sketch, *shards = lax.optimization_barrier((leaving, sketch, *shards))

    def for_z(step):
        return lax.dynamic_index_in_dim(leaving, (z + step) % NZ, 1, keepdims=False)

    far = for_z(4)
    goes_up = col(far[:, : np_ // 2], Z_UP)
    goes_down = col(far[:, np_ // 2 :], Z_DOWN)

    pivot_rows, sums_part = project(slot, slab, sketch_op, shards)
    goes_up, goes_down, sums_part = lax.optimization_barrier((goes_up, goes_down, sums_part))
    sums = exchange_sum(sums_part, "row")
    gram = spread_rows(sums[:, :np_])
    sums, gram = lax.optimization_barrier((sums, gram))
    inverse = inverse_factor(gram)
    by_goal = (
        ((dest * DEST_CAP + dest_rank)[None, :] == jnp.arange(ncol * DEST_CAP)[:, None])
        & goes[None, :]
    ).astype(F32)
    taken = (home[:, None] == cols[None, :]).astype(F32)
    pieces = jnp.concatenate([sums[:, 2 * np_ :], sketch_part], axis=0)
    small = pieces.shape[0] // 2
    sent = dot(by_goal, dot(taken, pieces, 1, 1), 1, 0)
    sent = sent.reshape(ncol, DEST_CAP, pieces.shape[0])
    new_sums = jnp.sum(lax.all_to_all(sent, "col", 0, 0), axis=0).T
    rest = spread_rows(
        jnp.concatenate([sums[:, np_:], new_sums[:small], new_sums[small:]], axis=1)
    )
    pivot_sketch, product = rest[:, :np_], rest[:, np_ : np_ + width]
    late = rest[:, np_ + width :]
    new_product, new_sketch = late[:, :DEST_CAP], late[:, DEST_CAP:]

    zero = jnp.zeros_like(goes_up)
    goes_up = for_z(3) + jnp.concatenate([goes_up, zero], axis=1)
    goes_down = for_z(-3) + jnp.concatenate([zero, goes_down], axis=1)
    for step in (2, 1):
        goes_up = for_z(step) + col(goes_up, Z_UP)
        goes_down = for_z(-step) + col(goes_down, Z_DOWN)
    arrived = for_z(0) + col(goes_up, Z_UP) + col(goes_down, Z_DOWN)
    keep = lax.dynamic_index_in_dim(arrived, xhi, 0, keepdims=False)
    give = lax.dynamic_index_in_dim(arrived, 1 - xhi, 0, keepdims=False)
    arrived = keep + col(give, XH_SWAP)
    outgoing = dot(by_goal, arrived, 1, 0).reshape(ncol, DEST_CAP, chunk)
    incoming = lax.all_to_all(outgoing, "col", 0, 0)
    new_rows = jnp.swapaxes(incoming, 0, 1).reshape(DEST_CAP, rows)

    in0 = cols // pw == block_order[0]
    in1 = cols // pw == block_order[1]
    at = (goal[:, None] == cols[None, :]) & goes[:, None]
    is_new = jnp.any(at, axis=0)
    slot_of = jnp.sum(jnp.where(at, dest_rank[:, None], 0), axis=0)
    put_new = (jnp.arange(DEST_CAP)[:, None] == slot_of[None, :]) & is_new[None, :]
    which = jnp.arange(np_, dtype=jnp.int32)
    put_pivot = (home[:, None] == cols[None, :])
    at0 = at & (which < pw)[:, None]
    is_new0 = jnp.any(at0, axis=0)
    put_new0 = put_new & is_new0[None, :]
    met = (pivots[1][:, None] == cols[None, :]) & hit[:, None]
    put_pivot0 = jnp.concatenate([put_pivot[:pw], met], axis=0)
    is_old0 = ~(is_new0 | in0 | jnp.any(met, axis=0))
    is_old = ~(is_new | in0 | in1)

    first_source = jnp.concatenate([new_product, gram], axis=1)
    put = jnp.concatenate([put_new, put_pivot], axis=0).astype(F32)
    put0 = jnp.concatenate([put_new0, put_pivot0], axis=0).astype(F32)
    before = jnp.where(is_old0[None, :], product, 0.0) + dot(first_source, put0, 1, 0)
    after = jnp.where(is_old[None, :], product, 0.0) + dot(first_source, put, 1, 0)
    top = dot(inverse[:pw], before, 1, 0)
    solved = dot(inverse, after, 1, 0)
    done = in0 | in1
    low = jnp.where(in0[None, :], 0.0, solved[pw:])
    factors = jnp.concatenate([top, low], axis=0)
    weights = jnp.concatenate(
        [
            jnp.where(in0[None, :], 0.0, solved[:pw]),
            jnp.where(done[None, :], 0.0, solved[pw:]),
        ],
        axis=0,
    )
    weights = dot(inverse, weights, 0, 0)
    mix = put - jnp.concatenate([jnp.zeros((DEST_CAP, width), F32), weights], axis=0)
    both_rows = jnp.concatenate([new_rows, pivot_rows], axis=0)
    slab_out = jnp.where(is_old[None, :], slab, 0.0) + dot(both_rows, mix, 0, 0, lax.Precision.HIGH)
    both_sketch = jnp.concatenate([new_sketch, pivot_sketch], axis=1)
    sketch_out = jnp.where(is_old[None, :], sketch, 0.0) + dot(both_sketch, mix, 1, 0, lax.Precision.HIGH)
    sketch_out = jnp.where(done[None, :], 0.0, sketch_out)
    return slab_out, factors, sketch_out


def local(slab, sketch_op, block_order, pivots):
    *planned, fits = plan(block_order, pivots, slab.shape[1])
    return lax.cond(
        fits,
        lambda *a: joint(*a),
        lambda *a: general(*a[:-1]),
        slab,
        sketch_op,
        block_order,
        pivots,
        planned,
    )


def solution(mesh):
    return jax.shard_map(
        local,
        mesh=mesh,
        in_specs=(P("row", "col"), P(None, "row"), P(), P()),
        out_specs=(P("row", "col"), P(None, "col"), P(None, "col")),
        check_vma=False,
    )
```

```python
import jax
import jax.numpy as jnp
from jax import lax
from jax.experimental import pallas as pl
from jax.experimental.pallas import tpu as pltpu
from jax.sharding import PartitionSpec as P


HI = lax.Precision.HIGHEST
F32 = jnp.float32

NX, NY, NCORE, NXH, NZ = 2, 4, 2, 2, 8
PAIR_CAP = 56
DEST_CAP = 32


def dot(a, b, ca, cb, precision=HI):
    return lax.dot_general(
        a, b, (((ca,), (cb,)), ((), ())), precision=precision, preferred_element_type=F32
    )


BLOCK = 128
SHIFT = 9
STRIP = 16
VM = pl.BlockSpec(memory_space=pltpu.VMEM)
BF16 = jnp.bfloat16


def split2(x):
    high = x.astype(BF16)
    return high, (x - high.astype(F32)).astype(BF16)


def split3(x):
    high, rest = x.astype(BF16), None
    left = x - high.astype(F32)
    middle = left.astype(BF16)
    rest = (left - middle.astype(F32)).astype(BF16)
    return high, middle, rest


def dot3(a, b, ca, cb):
    a0, a1 = a
    b0, b1 = b
    return (
        dot(a0, b1, ca, cb, None) + dot(a1, b0, ca, cb, None)
    ) + dot(a0, b0, ca, cb, None)


def factor_block(s_ref, w_ref, n):
    sub = lax.broadcasted_iota(jnp.int32, (STRIP, n), 0)
    w_ref[...] = (
        lax.broadcasted_iota(jnp.int32, (n, n), 0) == lax.broadcasted_iota(jnp.int32, (n, n), 1)
    ).astype(F32)
    for start in range(0, n, STRIP):
        stop = start + STRIP
        v = s_ref[start:stop, :]
        w = w_ref[start:stop, :]
        lanes = [jnp.broadcast_to(v[:, start + m : start + m + 1], (STRIP, n)) for m in range(STRIP)]
        scale = jnp.zeros((STRIP, n), F32)
        for i in range(STRIP):
            pivot = lanes[i][i : i + 1, :]
            scale = jnp.where(sub == i, pivot, scale)
            if i == STRIP - 1:
                break
            f = jnp.where(sub > i, lanes[i] * (1.0 / pivot), 0.0)
            for m in range(i + 1, STRIP):
                lanes[m] = lanes[m] - f * lanes[m][i : i + 1, :]
            v = v - f * v[i : i + 1, :]
            w = w - f * w[i : i + 1, :]
        root = 1.0 / jnp.sqrt(scale)
        v, w = v * root, w * root
        w_ref[start:stop, :] = w
        if stop < n:
            update = dot(v, jnp.concatenate([v, w], axis=1), 0, 0)
            s_ref[stop:, :] = s_ref[stop:, :] - update[stop:, :n]
            w_ref[stop:, :] = w_ref[stop:, :] - update[stop:, n:]


def inverse_factor_kernel(gram_ref, out_ref, s_ref, w_ref):
    n = s_ref.shape[0]
    s_ref[...] = gram_ref[:n, :n]
    factor_block(s_ref, w_ref, n)
    inv0 = w_ref[...]
    if gram_ref.shape[0] == n:
        out_ref[...] = inv0
        return
    cross = dot(gram_ref[n:, :n], inv0, 1, 1)
    out_ref[:n, :n] = inv0
    out_ref[:n, n:] = jnp.zeros((n, n), F32)
    s_ref[...] = gram_ref[n:, n:] - dot(cross, cross, 1, 1)
    lead = dot(cross, inv0, 1, 0)
    factor_block(s_ref, w_ref, n)
    inv1 = w_ref[...]
    out_ref[n:, :n] = -dot(inv1, lead, 1, 0)
    out_ref[n:, n:] = inv1


def joint_factor_kernel(near_ref, other_ref, gram_ref, out_ref, s_ref, w_ref):
    here = lax.axis_index("row")
    core = lax.rem(here, NCORE)
    y = lax.rem(here // NCORE, NY)
    x = here // (NCORE * NY)
    m = 16
    for c, ref in enumerate((near_ref, other_ref)):
        for t in range(NX):
            for i in range(NY):
                chunk = ((x ^ t) * NY + lax.rem(y + i, NY)) * NCORE + (core ^ c)
                at = (t * NY + i) * m
                gram_ref[pl.ds(pl.multiple_of(chunk * m, m), m), :] = ref[at : at + m, :]
    inverse_factor_kernel(gram_ref, out_ref, s_ref, w_ref)


def joint_factor(mine):
    half = mine.shape[0] // 2
    up, down = row(mine, Y_UP), row(mine, Y_DOWN)
    far_top, far_low = row(up[:half], Y_UP), row(down[half:], Y_DOWN)
    ring = jnp.concatenate([mine, down, far_top, far_low, up], axis=0)
    near = jnp.concatenate([ring, row(ring, X_SWAP)], axis=0)
    other = row(near, CORE_SWAP)
    n = mine.shape[1]
    shape = jax.ShapeDtypeStruct((n, n), F32)
    return pl.pallas_call(
        joint_factor_kernel,
        out_shape=(shape, shape),
        in_specs=[VM, VM],
        out_specs=(VM, VM),
        scratch_shapes=[pltpu.VMEM((BLOCK, BLOCK), F32)] * 2,
        cost_estimate=pl.CostEstimate(
            flops=10_000_000_000, bytes_accessed=3 * n * n * 4, transcendentals=0
        ),
        name="joint_factor",
    )(near, other)


def inverse_factor(gram):
    n = gram.shape[0]
    return pl.pallas_call(
        inverse_factor_kernel,
        out_shape=jax.ShapeDtypeStruct((n, n), F32),
        in_specs=[VM],
        out_specs=VM,
        scratch_shapes=[pltpu.VMEM((BLOCK, BLOCK), F32)] * 2,
        cost_estimate=pl.CostEstimate(flops=20_000_000, bytes_accessed=2 * n * n * 4, transcendentals=0),
        name="inverse_factor",
    )(gram)


def plan_kernel(order_ref, pivots_ref, table_ref, columns_ref, fits_ref):
    place = lax.axis_index("col")
    z = lax.rem(place, NZ)
    pw, wide = BLOCK, 2 * BLOCK
    pivots = pivots_ref[...]
    pivot_cols = jnp.concatenate([pivots.astype(F32), jnp.zeros((pw - 2, pw), F32)], axis=0)
    pivot_cols = pivot_cols.T.astype(jnp.int32)
    first, second = pivots[0:1, :], pivots[1:2, :]
    sub = lax.broadcasted_iota(jnp.int32, (pw, pw), 0)
    lane = lax.broadcasted_iota(jnp.int32, (1, pw), 1)
    meet = pivot_cols[:, 0:1] == second
    met_by = pivot_cols[:, 1:2] == first
    hit = jnp.sum(meet.astype(jnp.int32), axis=0, keepdims=True)
    lost = jnp.sum(met_by.astype(jnp.int32), axis=0, keepdims=True)
    start0, start1 = order_ref[0] * pw, order_ref[1] * pw
    moved = start0 + jnp.sum(jnp.where(meet, sub, 0), axis=0, keepdims=True)
    source = jnp.concatenate([first, jnp.where(hit > 0, moved, second)], axis=1)
    home = jnp.concatenate([start0 + lane, start1 + lane], axis=1)
    goal = jnp.concatenate([first, second], axis=1)
    goes = jnp.concatenate([1 - lost, jnp.ones_like(lost)], axis=1)
    met = jnp.concatenate([jnp.zeros_like(hit), hit], axis=1)
    pair = (source >> SHIFT) & (NZ - 1)
    dest = jnp.where(goes > 0, goal >> SHIFT, -1)
    blank = jnp.zeros((pw - 2, wide), F32)
    groups = jnp.concatenate([pair.astype(F32), dest.astype(F32), blank], axis=0).T
    groups = groups.astype(jnp.int32)
    earlier = lax.broadcasted_iota(jnp.int32, (wide, wide), 0) < lax.broadcasted_iota(
        jnp.int32, (wide, wide), 1
    )
    pair_rank = jnp.sum(
        ((groups[:, 0:1] == pair) & earlier).astype(jnp.int32), axis=0, keepdims=True
    )
    dest_rank = jnp.sum(
        ((groups[:, 1:2] == dest) & earlier).astype(jnp.int32), axis=0, keepdims=True
    )
    slot = ((z - pair) & (NZ - 1)) * PAIR_CAP + pair_rank
    table = jnp.concatenate([source, pair_rank, home, goal, goes, dest_rank, met, slot], axis=0)
    table_ref[...] = table
    rows = jnp.concatenate([table.astype(F32), jnp.zeros((pw - 8, wide), F32)], axis=0)
    columns_ref[...] = rows.T.astype(jnp.int32)
    most = jnp.maximum(
        jnp.max(pair_rank) - PAIR_CAP, jnp.max(jnp.where(goes > 0, dest_rank, 0)) - DEST_CAP
    )
    fits_ref[0] = (most < 0).astype(jnp.int32)


def plan(block_order, pivots):
    wide = 2 * BLOCK
    smem = pl.BlockSpec(memory_space=pltpu.SMEM)
    shape = jax.ShapeDtypeStruct
    return pl.pallas_call(
        plan_kernel,
        out_shape=(
            shape((8, wide), jnp.int32),
            shape((wide, BLOCK), jnp.int32),
            shape((1,), jnp.int32),
        ),
        in_specs=[smem, VM],
        out_specs=(VM, VM, smem),
        name="plan",
    )(block_order, pivots)


def pack_kernel(table_ref, slab_ref, out_ref):
    slots, width = out_ref.shape[0], slab_ref.shape[1]
    place = lax.axis_index("col")
    source, rank = table_ref[0:1, :], table_ref[1:2, :]
    slot = lax.broadcasted_iota(jnp.int32, (slots, source.shape[1]), 0)
    mine = (rank == slot) & ((source >> SHIFT) == place)
    at = jnp.sum(jnp.where(mine, source - place * width + 1, 0), axis=1, keepdims=True) - 1
    take = (at == lax.broadcasted_iota(jnp.int32, (slots, width), 1)).astype(F32).astype(BF16)
    pieces = split3(slab_ref[...])
    out_ref[...] = sum(dot(take, p, 1, 1, None) for p in pieces[::-1])


def pack(table, slab):
    (rows, width), step = slab.shape, 256
    return pl.pallas_call(
        pack_kernel,
        out_shape=jax.ShapeDtypeStruct((PAIR_CAP, rows), F32),
        grid=(rows // step,),
        in_specs=[VM, pl.BlockSpec((step, width), lambda k: (k, 0))],
        out_specs=pl.BlockSpec((PAIR_CAP, step), lambda k: (0, k)),
        cost_estimate=pl.CostEstimate(
            flops=6 * PAIR_CAP * slab.size, bytes_accessed=8 * slab.size, transcendentals=0
        ),
        name="pack",
    )(table, slab)


def leave_kernel(order_ref, slab_ref, out_ref):
    place = lax.axis_index("col")
    for k in range(2):
        rows = slice(k * BLOCK, (k + 1) * BLOCK)
        start = order_ref[k] * BLOCK
        owned = (start >> SHIFT) == place

        @pl.when(owned)
        def _():
            offset = pl.multiple_of(start - place * slab_ref.shape[1], BLOCK)
            for m in range(out_ref.shape[0]):
                part = slice(m * BLOCK, (m + 1) * BLOCK)
                out_ref[m, rows, :] = slab_ref[part, pl.ds(offset, BLOCK)].T

        @pl.when(jnp.logical_not(owned))
        def _():
            out_ref[:, rows, :] = jnp.zeros((out_ref.shape[0], BLOCK, BLOCK), F32)


def leave(order, slab, chunks):
    (rows, width), some = slab.shape, 4
    return pl.pallas_call(
        leave_kernel,
        out_shape=jax.ShapeDtypeStruct((chunks, 2 * BLOCK, rows // chunks), F32),
        grid=(chunks // some,),
        in_specs=[
            pl.BlockSpec(memory_space=pltpu.SMEM),
            pl.BlockSpec((some * BLOCK, width), lambda k: (k, 0)),
        ],
        out_specs=pl.BlockSpec((some, 2 * BLOCK, BLOCK), lambda k: (k, 0, 0)),
        cost_estimate=pl.CostEstimate(
            flops=slab.size, bytes_accessed=6 * slab.size, transcendentals=0
        ),
        name="leave",
    )(order, slab)


def project_kernel(columns_ref, slab_ref, op_ref, *refs):
    *shards, rows_ref, sums_ref, all_ref = refs
    count, total = columns_ref.shape[0], all_ref.shape[0]
    start = 0
    for shard in shards:
        all_ref[start : start + shard.shape[0], :] = shard[...]
        start += shard.shape[0]
    spread = (
        columns_ref[:, 7:8] == lax.broadcasted_iota(jnp.int32, (count, total), 1)
    ).astype(F32).astype(BF16)

    @pl.when(pl.program_id(0) == 0)
    def _():
        sums_ref[...] = jnp.zeros(sums_ref.shape, F32)

    pieces = split3(all_ref[...])
    pivot = sum(dot(spread, p, 1, 0, None) for p in pieces[::-1])
    rows_ref[...] = pivot
    two = split2(pivot)
    sums_ref[:, :count] += dot(pivot, pivot, 1, 1)
    sums_ref[:, count : 2 * count] += dot3(split2(op_ref[...]), two, 1, 1)
    sums_ref[:, 2 * count :] += dot3(two, split2(slab_ref[...]), 1, 0)


def project(columns, slab, sketch_op, shards):
    count, (rows, width), step = columns.shape[0], slab.shape, 256
    total = sum(s.shape[0] for s in shards)
    across = lambda n: pl.BlockSpec((n, step), lambda k: (0, k))
    shape = jax.ShapeDtypeStruct
    return pl.pallas_call(
        project_kernel,
        out_shape=(
            shape((count, rows), F32),
            shape((count, 2 * count + width), F32),
        ),
        grid=(rows // step,),
        in_specs=[
            VM,
            pl.BlockSpec((step, width), lambda k: (k, 0)),
            across(sketch_op.shape[0]),
            *(across(s.shape[0]) for s in shards),
        ],
        out_specs=(
            across(count),
            pl.BlockSpec((count, 2 * count + width), lambda k: (0, 0)),
        ),
        scratch_shapes=[pltpu.VMEM((total, step), F32)],
        cost_estimate=pl.CostEstimate(
            flops=6 * count * rows * (total + 2 * count + width),
            bytes_accessed=4 * (slab.size + sketch_op.size + total * rows + count * rows),
            transcendentals=0,
        ),
        name="project",
    )(columns, slab, sketch_op, *shards)


def sketch_kernel(op_ref, slab_ref, out_ref):
    @pl.when(pl.program_id(0) == 0)
    def _():
        out_ref[...] = jnp.zeros(out_ref.shape, F32)

    out_ref[...] += dot3(split2(op_ref[...]), split2(slab_ref[...]), 1, 0)


def sketch_sum(sketch_op, slab):
    count, (rows, width), step = sketch_op.shape[0], slab.shape, 512
    return pl.pallas_call(
        sketch_kernel,
        out_shape=jax.ShapeDtypeStruct((count, width), F32),
        grid=(rows // step,),
        in_specs=[
            pl.BlockSpec((count, step), lambda k: (0, k)),
            pl.BlockSpec((step, width), lambda k: (k, 0)),
        ],
        out_specs=pl.BlockSpec((count, width), lambda k: (0, 0)),
        cost_estimate=pl.CostEstimate(
            flops=6 * count * slab.size,
            bytes_accessed=4 * (slab.size + sketch_op.size),
            transcendentals=0,
        ),
        name="sketch_sum",
    )(sketch_op, slab)


def row_perm(f):
    out = []
    for x in range(NX):
        for y in range(NY):
            for c in range(NCORE):
                u, v, w = f(x, y, c)
                out.append(((x * NY + y) * NCORE + c, (u * NY + v % NY) * NCORE + w))
    return out


def col_perm(f):
    out = []
    for x in range(NXH):
        for z in range(NZ):
            u, v = f(x, z)
            out.append((x * NZ + z, u * NZ + v % NZ))
    return out


Y_UP = row_perm(lambda x, y, c: (x, y + 1, c))
Y_DOWN = row_perm(lambda x, y, c: (x, y - 1, c))
X_SWAP = row_perm(lambda x, y, c: (1 - x, y, c))
CORE_SWAP = row_perm(lambda x, y, c: (x, y, 1 - c))
Z_UP = col_perm(lambda x, z: (x, z + 1))
Z_DOWN = col_perm(lambda x, z: (x, z - 1))
XH_SWAP = col_perm(lambda x, z: (1 - x, z))


def row(x, perm):
    return lax.ppermute(x, "row", perm)


def col(x, perm):
    return lax.ppermute(x, "col", perm)


def exchange_sum(x, axis):
    n = lax.axis_size(axis)
    parts = x.reshape(n, x.shape[0] // n, *x.shape[1:])
    return jnp.sum(lax.all_to_all(parts, axis, 0, 0), axis=0)


def all_sum(x, axis):
    n = lax.axis_size(axis)
    mine = exchange_sum(x, axis)
    spread = jnp.broadcast_to(mine[None], (n, *mine.shape))
    return lax.all_to_all(spread, axis, 0, 0).reshape(x.shape)


def spread_rows(x):
    n = lax.axis_size("row")
    copies = jnp.broadcast_to(x[None], (n, *x.shape))
    return lax.all_to_all(copies, "row", 0, 0).reshape(n * x.shape[0], x.shape[1])


def general(slab, sketch_op, block_order, pivots):
    width, pw = slab.shape[1], pivots.shape[1]
    place = lax.axis_index("col")
    base = place * width
    cols = base + jnp.arange(width, dtype=jnp.int32)
    sketch = all_sum(dot(sketch_op, slab, 1, 0), "row")

    def panel(k, carry):
        slab, sketch, finished, factors = carry
        start = block_order[k] * pw
        owner = start // width
        offset = start - owner * width
        owns = place == owner
        local = pivots[k] - base
        selector = (jnp.arange(width)[:, None] == local[None, :]).astype(F32)
        targeted = jnp.sum(selector, axis=1) > 0.5
        both = jnp.concatenate([slab, sketch])
        block = lax.dynamic_slice_in_dim(both, offset, pw, 1)
        moved = jnp.concatenate(
            [dot(both, selector, 1, 0), jnp.where(owns, block, 0.0)], axis=1
        )
        moved = all_sum(moved, "col")
        panel_cols, displaced = moved[:, :pw], moved[:, pw:]
        both = lax.dynamic_update_slice_in_dim(
            both, jnp.where(owns, panel_cols, block), offset, 1
        )
        both = jnp.where(targeted[None, :], dot(displaced, selector, 1, 1), both)
        slab, sketch = both[: slab.shape[0]], both[slab.shape[0] :]
        panel_slab, panel_sketch = panel_cols[: slab.shape[0]], panel_cols[slab.shape[0] :]
        gram = all_sum(dot(panel_slab, panel_slab, 0, 0), "row")
        inverse = inverse_factor(gram)
        basis = dot(panel_slab, inverse, 1, 1)
        projected = all_sum(dot(basis, slab, 0, 0), "row")
        factors = lax.dynamic_update_slice_in_dim(
            factors, jnp.where(finished[None, :], 0.0, projected), k * pw, 0
        )
        finished = finished | (cols // pw == block_order[k])
        slab = jnp.where(finished[None, :], slab, slab - dot(basis, projected, 1, 0))
        update = dot(dot(panel_sketch, inverse, 1, 1), projected, 1, 0)
        sketch = jnp.where(finished[None, :], 0.0, sketch - update)
        return slab, sketch, finished, factors

    carry = (
        slab,
        sketch,
        jnp.zeros((width,), dtype=bool),
        jnp.zeros((pivots.shape[0] * pw, width), F32),
    )
    slab, sketch, _, factors = lax.fori_loop(0, pivots.shape[0], panel, carry)
    return slab, factors, sketch


def joint(slab, sketch_op, block_order, pivots, table, columns):
    rows, width = slab.shape
    pw = pivots.shape[1]
    np_ = 2 * pw
    ncol = NXH * NZ
    place = lax.axis_index("col")
    z, xhi = place % NZ, place // NZ
    cols = place * width + jnp.arange(width, dtype=jnp.int32)
    home, goal, goes, dest_rank = table[2], table[3], table[4] > 0, table[5]
    hit = table[6, pw:] > 0
    dest = goal // width

    packed = pack(table, slab)
    sketch_part = sketch_sum(sketch_op, slab)
    shard = packed + col(packed, XH_SWAP)
    shard, sketch_part = lax.optimization_barrier((shard, sketch_part))
    half = PAIR_CAP // 2 // 8 * 8
    up1, down1 = col(shard, Z_UP), col(shard, Z_DOWN)
    chunk = rows // ncol
    leaving = leave(block_order, slab, ncol).reshape(NXH, NZ, np_, chunk)
    up1, down1, leaving = lax.optimization_barrier((up1, down1, leaving))
    up2, down2 = col(up1, Z_UP), col(down1, Z_DOWN)
    sketch_part = exchange_sum(sketch_part, "row")
    up3, down3 = col(up2, Z_UP), col(down2, Z_DOWN)
    up3, down3, sketch_part = lax.optimization_barrier((up3, down3, sketch_part))
    up4, down4 = col(up3[:half], Z_UP), col(down3[half:], Z_DOWN)
    sketch = spread_rows(sketch_part)

    shards = (shard, up1, up2, up3, up4, down4, down3, down2, down1)
    pivot_rows, sums_part = project(columns, slab, sketch_op, shards)
    leaving, sums_part = lax.optimization_barrier((leaving, sums_part))
    sums = exchange_sum(sums_part, "row")

    def for_z(step):
        return lax.dynamic_index_in_dim(leaving, (z + step) % NZ, 1, keepdims=False)

    far = for_z(4)
    goes_up = col(far[:, : np_ // 2], Z_UP)
    goes_down = col(far[:, np_ // 2 :], Z_DOWN)
    goes_up, goes_down = lax.optimization_barrier((goes_up, goes_down))

    gram, inverse = joint_factor(sums[:, :np_])
    by_goal = (
        ((dest * DEST_CAP + dest_rank)[None, :] == jnp.arange(ncol * DEST_CAP)[:, None])
        & goes[None, :]
    ).astype(F32)
    taken = (home[:, None] == cols[None, :]).astype(F32)
    pieces = jnp.concatenate([sums[:, 2 * np_ :], sketch_part], axis=0)
    small = pieces.shape[0] // 2
    sent = dot(by_goal, dot(taken, pieces, 1, 1), 1, 0)
    sent = sent.reshape(ncol, DEST_CAP, pieces.shape[0])
    sent = lax.all_to_all(sent, "col", 0, 0)
    new_sums = jnp.sum(sent, axis=0).T
    rest = jnp.concatenate([sums[:, np_:], new_sums[:small], new_sums[small:]], axis=1)
    rest = spread_rows(rest)
    pivot_sketch, product = rest[:, :np_], rest[:, np_ : np_ + width]
    late = rest[:, np_ + width :]
    new_product, new_sketch = late[:, :DEST_CAP], late[:, DEST_CAP:]

    zero = jnp.zeros_like(goes_up)
    goes_up = for_z(3) + jnp.concatenate([goes_up, zero], axis=1)
    goes_down = for_z(-3) + jnp.concatenate([zero, goes_down], axis=1)
    for step in (2, 1, 0):
        goes_up, goes_down = col(goes_up, Z_UP), col(goes_down, Z_DOWN)
        goes_up, goes_down = lax.optimization_barrier((goes_up, goes_down))
        if step > 0:
            goes_up, goes_down = for_z(step) + goes_up, for_z(-step) + goes_down
    arrived = for_z(0) + goes_up + goes_down
    keep = lax.dynamic_index_in_dim(arrived, xhi, 0, keepdims=False)
    give = lax.dynamic_index_in_dim(arrived, 1 - xhi, 0, keepdims=False)
    arrived = keep + col(give, XH_SWAP)
    outgoing = dot(by_goal, arrived, 1, 0).reshape(ncol, DEST_CAP, chunk)
    incoming = lax.all_to_all(outgoing, "col", 0, 0)
    new_rows = jnp.swapaxes(incoming, 0, 1).reshape(DEST_CAP, rows)

    in0 = cols // pw == block_order[0]
    in1 = cols // pw == block_order[1]
    at = (goal[:, None] == cols[None, :]) & goes[:, None]
    is_new = jnp.any(at, axis=0)
    slot_of = jnp.sum(jnp.where(at, dest_rank[:, None], 0), axis=0)
    put_new = (jnp.arange(DEST_CAP)[:, None] == slot_of[None, :]) & is_new[None, :]
    which = jnp.arange(np_, dtype=jnp.int32)
    put_pivot = (home[:, None] == cols[None, :])
    at0 = at & (which < pw)[:, None]
    is_new0 = jnp.any(at0, axis=0)
    put_new0 = put_new & is_new0[None, :]
    met = (pivots[1][:, None] == cols[None, :]) & hit[:, None]
    put_pivot0 = jnp.concatenate([put_pivot[:pw], met], axis=0)
    is_old0 = ~(is_new0 | in0 | jnp.any(met, axis=0))
    is_old = ~(is_new | in0 | in1)

    first_source = jnp.concatenate([new_product, gram], axis=1)
    put = jnp.concatenate([put_new, put_pivot], axis=0).astype(F32)
    put0 = jnp.concatenate([put_new0, put_pivot0], axis=0).astype(F32)
    before = jnp.where(is_old0[None, :], product, 0.0) + dot(first_source, put0, 1, 0)
    after = jnp.where(is_old[None, :], product, 0.0) + dot(first_source, put, 1, 0)
    top = dot(inverse[:pw], before, 1, 0)
    solved = dot(inverse, after, 1, 0)
    done = in0 | in1
    low = jnp.where(in0[None, :], 0.0, solved[pw:])
    factors = jnp.concatenate([top, low], axis=0)
    weights = jnp.concatenate(
        [
            jnp.where(in0[None, :], 0.0, solved[:pw]),
            jnp.where(done[None, :], 0.0, solved[pw:]),
        ],
        axis=0,
    )
    weights = dot(inverse, weights, 0, 0)
    mix = put - jnp.concatenate([jnp.zeros((DEST_CAP, width), F32), weights], axis=0)
    both_rows = jnp.concatenate([new_rows, pivot_rows], axis=0)
    slab_out = jnp.where(is_old[None, :], slab, 0.0) + dot(both_rows, mix, 0, 0, lax.Precision.HIGH)
    both_sketch = jnp.concatenate([new_sketch, pivot_sketch], axis=1)
    sketch_out = jnp.where(is_old[None, :], sketch, 0.0) + dot(both_sketch, mix, 1, 0, lax.Precision.HIGH)
    sketch_out = jnp.where(done[None, :], 0.0, sketch_out)
    return slab_out, factors, sketch_out


def local(slab, sketch_op, block_order, pivots):
    table, columns, fits = plan(block_order, pivots)

    return lax.cond(
        fits[0] > 0,
        joint,
        lambda *a: general(*a[:4]),
        slab,
        sketch_op,
        block_order,
        pivots,
        table,
        columns,
    )


def solution(mesh):
    return jax.shard_map(
        local,
        mesh=mesh,
        in_specs=(P("row", "col"), P(None, "row"), P(), P()),
        out_specs=(P("row", "col"), P(None, "col"), P(None, "col")),
        check_vma=False,
    )
```

```python
import jax
import jax.numpy as jnp
from jax import lax
from jax.experimental import pallas as pl
from jax.experimental.pallas import tpu as pltpu
from jax.sharding import PartitionSpec as P


HI = lax.Precision.HIGHEST
F32 = jnp.float32

NX, NY, NCORE, NXH, NZ = 2, 4, 2, 2, 8
PAIR_CAP = 56
DEST_CAP = 32


def dot(a, b, ca, cb, precision=HI):
    return lax.dot_general(
        a, b, (((ca,), (cb,)), ((), ())), precision=precision, preferred_element_type=F32
    )


BLOCK = 128
SHIFT = 9
STRIP = 16
VM = pl.BlockSpec(memory_space=pltpu.VMEM)
BF16 = jnp.bfloat16


def split2(x):
    high = x.astype(BF16)
    return high, (x - high.astype(F32)).astype(BF16)


def split3(x):
    high, rest = x.astype(BF16), None
    left = x - high.astype(F32)
    middle = left.astype(BF16)
    rest = (left - middle.astype(F32)).astype(BF16)
    return high, middle, rest


def dot3(a, b, ca, cb):
    a0, a1 = a
    b0, b1 = b
    return (
        dot(a0, b1, ca, cb, None) + dot(a1, b0, ca, cb, None)
    ) + dot(a0, b0, ca, cb, None)


def dot6(a, b):
    terms = ((0, 2), (2, 0), (1, 1), (0, 1), (1, 0), (0, 0))
    return sum(dot(a[i], b[j], 1, 0, None) for i, j in terms)


def factor_block(s_ref, w_ref, n):
    sub = lax.broadcasted_iota(jnp.int32, (STRIP, n), 0)
    lane = lax.broadcasted_iota(jnp.int32, (STRIP, n), 1)
    w_ref[...] = (
        lax.broadcasted_iota(jnp.int32, (n, n), 0) == lax.broadcasted_iota(jnp.int32, (n, n), 1)
    ).astype(F32)

    @pl.loop(0, n // STRIP)
    def _(k):
        start = pl.multiple_of(k * STRIP, STRIP)
        v = s_ref[pl.ds(start, STRIP), :]
        w = w_ref[pl.ds(start, STRIP), :]
        turned = pltpu.roll(v, lax.rem(n - start, n), 1)
        lanes = [jnp.broadcast_to(turned[:, m : m + 1], (STRIP, n)) for m in range(STRIP)]
        scale = jnp.zeros((STRIP, n), F32)
        for i in range(STRIP):
            pivot = lanes[i][i : i + 1, :]
            scale = jnp.where(sub == i, pivot, scale)
            if i == STRIP - 1:
                break
            f = jnp.where(sub > i, lanes[i] * (1.0 / pivot), 0.0)
            for m in range(i + 1, STRIP):
                lanes[m] = lanes[m] - f * lanes[m][i : i + 1, :]
            v = v - f * v[i : i + 1, :]
            w = w - f * w[i : i + 1, :]
        root = 1.0 / jnp.sqrt(scale)
        v, w = v * root, w * root
        w_ref[pl.ds(start, STRIP), :] = w
        below = jnp.where(lane >= start + STRIP, v, 0.0)
        update = dot(below, jnp.concatenate([v, w], axis=1), 0, 0)
        s_ref[...] = s_ref[...] - update[:, :n]
        w_ref[...] = w_ref[...] - update[:, n:]


def inverse_factor_kernel(gram_ref, out_ref, s_ref, w_ref):
    n = s_ref.shape[0]
    s_ref[...] = gram_ref[:n, :n]
    factor_block(s_ref, w_ref, n)
    inv0 = w_ref[...]
    if gram_ref.shape[0] == n:
        out_ref[...] = inv0
        return
    cross = dot(gram_ref[n:, :n], inv0, 1, 1)
    out_ref[:n, :n] = inv0
    out_ref[:n, n:] = jnp.zeros((n, n), F32)
    s_ref[...] = gram_ref[n:, n:] - dot(cross, cross, 1, 1)
    lead = dot(cross, inv0, 1, 0)
    factor_block(s_ref, w_ref, n)
    inv1 = w_ref[...]
    out_ref[n:, :n] = -dot(inv1, lead, 1, 0)
    out_ref[n:, n:] = inv1


def joint_factor_kernel(near_ref, other_ref, gram_ref, out_ref, s_ref, w_ref):
    here = lax.axis_index("row")
    core = lax.rem(here, NCORE)
    y = lax.rem(here // NCORE, NY)
    x = here // (NCORE * NY)
    m = 16
    for c, ref in enumerate((near_ref, other_ref)):
        for t in range(NX):
            for i in range(NY):
                chunk = ((x ^ t) * NY + lax.rem(y + i, NY)) * NCORE + (core ^ c)
                at = (t * NY + i) * m
                gram_ref[pl.ds(pl.multiple_of(chunk * m, m), m), :] = ref[at : at + m, :]
    inverse_factor_kernel(gram_ref, out_ref, s_ref, w_ref)


def joint_factor(mine):
    half = mine.shape[0] // 2
    up = row(mine, Y_UP)
    down = row(mine, Y_DOWN)
    up, down = lax.optimization_barrier((up, down))
    far_top = row(up[:half], Y_UP)
    far_low = row(down[half:], Y_DOWN)
    ring = jnp.concatenate([mine, down, far_top, far_low, up], axis=0)
    near = jnp.concatenate([ring, row(ring, X_SWAP)], axis=0)
    other = row(near, CORE_SWAP)
    n = mine.shape[1]
    shape = jax.ShapeDtypeStruct((n, n), F32)
    return pl.pallas_call(
        joint_factor_kernel,
        out_shape=(shape, shape),
        in_specs=[VM, VM],
        out_specs=(VM, VM),
        scratch_shapes=[pltpu.VMEM((BLOCK, BLOCK), F32)] * 2,
        cost_estimate=pl.CostEstimate(
            flops=10_000_000_000, bytes_accessed=3 * n * n * 4, transcendentals=0
        ),
        name="joint_factor",
    )(near, other)


def inverse_factor(gram):
    n = gram.shape[0]
    return pl.pallas_call(
        inverse_factor_kernel,
        out_shape=jax.ShapeDtypeStruct((n, n), F32),
        in_specs=[VM],
        out_specs=VM,
        scratch_shapes=[pltpu.VMEM((BLOCK, BLOCK), F32)] * 2,
        cost_estimate=pl.CostEstimate(flops=20_000_000, bytes_accessed=2 * n * n * 4, transcendentals=0),
        name="inverse_factor",
    )(gram)


def plan_kernel(order_ref, pivots_ref, table_ref, columns_ref, fits_ref):
    place = lax.axis_index("col")
    z = lax.rem(place, NZ)
    pw, wide = BLOCK, 2 * BLOCK
    pivots = pivots_ref[...]
    pivot_cols = jnp.concatenate([pivots.astype(F32), jnp.zeros((pw - 2, pw), F32)], axis=0)
    pivot_cols = pivot_cols.T.astype(jnp.int32)
    first, second = pivots[0:1, :], pivots[1:2, :]
    sub = lax.broadcasted_iota(jnp.int32, (pw, pw), 0)
    lane = lax.broadcasted_iota(jnp.int32, (1, pw), 1)
    meet = pivot_cols[:, 0:1] == second
    met_by = pivot_cols[:, 1:2] == first
    hit = jnp.sum(meet.astype(jnp.int32), axis=0, keepdims=True)
    lost = jnp.sum(met_by.astype(jnp.int32), axis=0, keepdims=True)
    start0, start1 = order_ref[0] * pw, order_ref[1] * pw
    moved = start0 + jnp.sum(jnp.where(meet, sub, 0), axis=0, keepdims=True)
    source = jnp.concatenate([first, jnp.where(hit > 0, moved, second)], axis=1)
    home = jnp.concatenate([start0 + lane, start1 + lane], axis=1)
    goal = jnp.concatenate([first, second], axis=1)
    goes = jnp.concatenate([1 - lost, jnp.ones_like(lost)], axis=1)
    met = jnp.concatenate([jnp.zeros_like(hit), hit], axis=1)
    pair = (source >> SHIFT) & (NZ - 1)
    dest = jnp.where(goes > 0, goal >> SHIFT, -1)
    blank = jnp.zeros((pw - 2, wide), F32)
    groups = jnp.concatenate([pair.astype(F32), dest.astype(F32), blank], axis=0).T
    groups = groups.astype(jnp.int32)
    earlier = lax.broadcasted_iota(jnp.int32, (wide, wide), 0) < lax.broadcasted_iota(
        jnp.int32, (wide, wide), 1
    )
    pair_rank = jnp.sum(
        ((groups[:, 0:1] == pair) & earlier).astype(jnp.int32), axis=0, keepdims=True
    )
    dest_rank = jnp.sum(
        ((groups[:, 1:2] == dest) & earlier).astype(jnp.int32), axis=0, keepdims=True
    )
    slot = ((z - pair) & (NZ - 1)) * PAIR_CAP + pair_rank
    table = jnp.concatenate([source, pair_rank, home, goal, goes, dest_rank, met, slot], axis=0)
    table_ref[...] = table
    rows = jnp.concatenate([table.astype(F32), jnp.zeros((pw - 8, wide), F32)], axis=0)
    columns_ref[...] = rows.T.astype(jnp.int32)
    most = jnp.maximum(
        jnp.max(pair_rank) - PAIR_CAP, jnp.max(jnp.where(goes > 0, dest_rank, 0)) - DEST_CAP
    )
    fits_ref[0] = (most < 0).astype(jnp.int32)


def plan(block_order, pivots):
    wide = 2 * BLOCK
    smem = pl.BlockSpec(memory_space=pltpu.SMEM)
    shape = jax.ShapeDtypeStruct
    return pl.pallas_call(
        plan_kernel,
        out_shape=(
            shape((8, wide), jnp.int32),
            shape((wide, BLOCK), jnp.int32),
            shape((1,), jnp.int32),
        ),
        in_specs=[smem, VM],
        out_specs=(VM, VM, smem),
        name="plan",
    )(block_order, pivots)


def pack_kernel(table_ref, slab_ref, out_ref):
    slots, width = out_ref.shape[0], slab_ref.shape[1]
    place = lax.axis_index("col")
    source, rank = table_ref[0:1, :], table_ref[1:2, :]
    slot = lax.broadcasted_iota(jnp.int32, (slots, source.shape[1]), 0)
    mine = (rank == slot) & ((source >> SHIFT) == place)
    at = jnp.sum(jnp.where(mine, source - place * width + 1, 0), axis=1, keepdims=True) - 1
    take = (at == lax.broadcasted_iota(jnp.int32, (slots, width), 1)).astype(F32).astype(BF16)
    pieces = split3(slab_ref[...])
    out_ref[...] = sum(dot(take, p, 1, 1, None) for p in pieces[::-1])


def pack(table, slab):
    (rows, width), step = slab.shape, 512
    return pl.pallas_call(
        pack_kernel,
        out_shape=jax.ShapeDtypeStruct((PAIR_CAP, rows), F32),
        grid=(rows // step,),
        in_specs=[VM, pl.BlockSpec((step, width), lambda k: (k, 0))],
        out_specs=pl.BlockSpec((PAIR_CAP, step), lambda k: (0, k)),
        cost_estimate=pl.CostEstimate(
            flops=6 * PAIR_CAP * slab.size, bytes_accessed=8 * slab.size, transcendentals=0
        ),
        name="pack",
    )(table, slab)


def leave_kernel(order_ref, slab_ref, out_ref):
    place = lax.axis_index("col")
    for k in range(2):
        rows = slice(k * BLOCK, (k + 1) * BLOCK)
        start = order_ref[k] * BLOCK
        owned = (start >> SHIFT) == place

        @pl.when(owned)
        def _():
            offset = pl.multiple_of(start - place * slab_ref.shape[1], BLOCK)
            for m in range(out_ref.shape[0]):
                part = slice(m * BLOCK, (m + 1) * BLOCK)
                out_ref[m, rows, :] = slab_ref[part, pl.ds(offset, BLOCK)].T

        @pl.when(jnp.logical_not(owned))
        def _():
            out_ref[:, rows, :] = jnp.zeros((out_ref.shape[0], BLOCK, BLOCK), F32)


def leave(order, slab, chunks):
    (rows, width), some = slab.shape, 4
    return pl.pallas_call(
        leave_kernel,
        out_shape=jax.ShapeDtypeStruct((chunks, 2 * BLOCK, rows // chunks), F32),
        grid=(chunks // some,),
        in_specs=[
            pl.BlockSpec(memory_space=pltpu.SMEM),
            pl.BlockSpec((some * BLOCK, width), lambda k: (k, 0)),
        ],
        out_specs=pl.BlockSpec((some, 2 * BLOCK, BLOCK), lambda k: (k, 0, 0)),
        cost_estimate=pl.CostEstimate(
            flops=slab.size, bytes_accessed=6 * slab.size, transcendentals=0
        ),
        name="leave",
    )(order, slab)


def project_kernel(columns_ref, slab_ref, op_ref, *refs):
    *shards, rows_ref, sums_ref, all_ref = refs
    count, total = columns_ref.shape[0], all_ref.shape[0]
    start = 0
    for shard in shards:
        all_ref[start : start + shard.shape[0], :] = shard[...]
        start += shard.shape[0]
    spread = (
        columns_ref[:, 7:8] == lax.broadcasted_iota(jnp.int32, (count, total), 1)
    ).astype(F32).astype(BF16)

    @pl.when(pl.program_id(0) == 0)
    def _():
        sums_ref[...] = jnp.zeros(sums_ref.shape, F32)

    pieces = split3(all_ref[...])
    pivot = sum(dot(spread, p, 1, 0, None) for p in pieces[::-1])
    rows_ref[...] = pivot
    three = split3(pivot)
    turned = [p.T for p in three]
    sums_ref[:, :count] += dot6(three, turned)
    sums_ref[:, count : 2 * count] += dot3(split2(op_ref[...]), turned[:2], 1, 0)
    sums_ref[:, 2 * count :] += dot3(three[:2], split2(slab_ref[...]), 1, 0)


def project(columns, slab, sketch_op, shards):
    count, (rows, width), step = columns.shape[0], slab.shape, 512
    total = sum(s.shape[0] for s in shards)
    across = lambda n: pl.BlockSpec((n, step), lambda k: (0, k))
    shape = jax.ShapeDtypeStruct
    return pl.pallas_call(
        project_kernel,
        out_shape=(
            shape((count, rows), F32),
            shape((count, 2 * count + width), F32),
        ),
        grid=(rows // step,),
        in_specs=[
            VM,
            pl.BlockSpec((step, width), lambda k: (k, 0)),
            across(sketch_op.shape[0]),
            *(across(s.shape[0]) for s in shards),
        ],
        out_specs=(
            across(count),
            pl.BlockSpec((count, 2 * count + width), lambda k: (0, 0)),
        ),
        scratch_shapes=[pltpu.VMEM((total, step), F32)],
        cost_estimate=pl.CostEstimate(
            flops=6 * count * rows * (total + 2 * count + width),
            bytes_accessed=4 * (slab.size + sketch_op.size + total * rows + count * rows),
            transcendentals=0,
        ),
        name="project",
    )(columns, slab, sketch_op, *shards)


def sketch_kernel(op_ref, slab_ref, out_ref):
    @pl.when(pl.program_id(0) == 0)
    def _():
        out_ref[...] = jnp.zeros(out_ref.shape, F32)

    out_ref[...] += dot3(split2(op_ref[...]), split2(slab_ref[...]), 1, 0)


def sketch_sum(sketch_op, slab):
    count, (rows, width), step = sketch_op.shape[0], slab.shape, 512
    return pl.pallas_call(
        sketch_kernel,
        out_shape=jax.ShapeDtypeStruct((count, width), F32),
        grid=(rows // step,),
        in_specs=[
            pl.BlockSpec((count, step), lambda k: (0, k)),
            pl.BlockSpec((step, width), lambda k: (k, 0)),
        ],
        out_specs=pl.BlockSpec((count, width), lambda k: (0, 0)),
        cost_estimate=pl.CostEstimate(
            flops=6 * count * slab.size,
            bytes_accessed=4 * (slab.size + sketch_op.size),
            transcendentals=0,
        ),
        name="sketch_sum",
    )(sketch_op, slab)


def row_perm(f):
    out = []
    for x in range(NX):
        for y in range(NY):
            for c in range(NCORE):
                u, v, w = f(x, y, c)
                out.append(((x * NY + y) * NCORE + c, (u * NY + v % NY) * NCORE + w))
    return out


def col_perm(f):
    out = []
    for x in range(NXH):
        for z in range(NZ):
            u, v = f(x, z)
            out.append((x * NZ + z, u * NZ + v % NZ))
    return out


Y_UP = row_perm(lambda x, y, c: (x, y + 1, c))
Y_DOWN = row_perm(lambda x, y, c: (x, y - 1, c))
X_SWAP = row_perm(lambda x, y, c: (1 - x, y, c))
CORE_SWAP = row_perm(lambda x, y, c: (x, y, 1 - c))
Z_UP = col_perm(lambda x, z: (x, z + 1))
Z_DOWN = col_perm(lambda x, z: (x, z - 1))
XH_SWAP = col_perm(lambda x, z: (1 - x, z))


def row(x, perm):
    return lax.ppermute(x, "row", perm)


def col(x, perm):
    return lax.ppermute(x, "col", perm)


def hold_kernel(in_ref, out_ref):
    out_ref[...] = in_ref[...]


def hold(x):
    block = pl.BlockSpec((128, 512), lambda i, j: (i, j))
    return pl.pallas_call(
        hold_kernel,
        out_shape=jax.ShapeDtypeStruct(x.shape, x.dtype),
        grid=(x.shape[0] // 128, x.shape[1] // 512),
        in_specs=[block],
        out_specs=block,
        name="hold",
    )(x)


def exchange_sum(x, axis):
    n = lax.axis_size(axis)
    parts = x.reshape(n, x.shape[0] // n, *x.shape[1:])
    return jnp.sum(lax.all_to_all(parts, axis, 0, 0), axis=0)


def all_sum(x, axis):
    n = lax.axis_size(axis)
    mine = exchange_sum(x, axis)
    spread = jnp.broadcast_to(mine[None], (n, *mine.shape))
    return lax.all_to_all(spread, axis, 0, 0).reshape(x.shape)


def spread_rows(x):
    n = lax.axis_size("row")
    copies = jnp.broadcast_to(x[None], (n, *x.shape))
    return lax.all_to_all(copies, "row", 0, 0).reshape(n * x.shape[0], x.shape[1])


def general(slab, sketch_op, block_order, pivots):
    width, pw = slab.shape[1], pivots.shape[1]
    place = lax.axis_index("col")
    base = place * width
    cols = base + jnp.arange(width, dtype=jnp.int32)
    sketch = all_sum(dot(sketch_op, slab, 1, 0), "row")

    def panel(k, carry):
        slab, sketch, finished, factors = carry
        start = block_order[k] * pw
        owner = start // width
        offset = start - owner * width
        owns = place == owner
        local = pivots[k] - base
        selector = (jnp.arange(width)[:, None] == local[None, :]).astype(F32)
        targeted = jnp.sum(selector, axis=1) > 0.5
        both = jnp.concatenate([slab, sketch])
        block = lax.dynamic_slice_in_dim(both, offset, pw, 1)
        moved = jnp.concatenate(
            [dot(both, selector, 1, 0), jnp.where(owns, block, 0.0)], axis=1
        )
        moved = all_sum(moved, "col")
        panel_cols, displaced = moved[:, :pw], moved[:, pw:]
        both = lax.dynamic_update_slice_in_dim(
            both, jnp.where(owns, panel_cols, block), offset, 1
        )
        both = jnp.where(targeted[None, :], dot(displaced, selector, 1, 1), both)
        slab, sketch = both[: slab.shape[0]], both[slab.shape[0] :]
        panel_slab, panel_sketch = panel_cols[: slab.shape[0]], panel_cols[slab.shape[0] :]
        gram = all_sum(dot(panel_slab, panel_slab, 0, 0), "row")
        inverse = inverse_factor(gram)
        basis = dot(panel_slab, inverse, 1, 1)
        projected = all_sum(dot(basis, slab, 0, 0), "row")
        factors = lax.dynamic_update_slice_in_dim(
            factors, jnp.where(finished[None, :], 0.0, projected), k * pw, 0
        )
        finished = finished | (cols // pw == block_order[k])
        slab = jnp.where(finished[None, :], slab, slab - dot(basis, projected, 1, 0))
        update = dot(dot(panel_sketch, inverse, 1, 1), projected, 1, 0)
        sketch = jnp.where(finished[None, :], 0.0, sketch - update)
        return slab, sketch, finished, factors

    carry = (
        slab,
        sketch,
        jnp.zeros((width,), dtype=bool),
        jnp.zeros((pivots.shape[0] * pw, width), F32),
    )
    slab, sketch, _, factors = lax.fori_loop(0, pivots.shape[0], panel, carry)
    return slab, factors, sketch


def joint(slab, sketch_op, block_order, pivots, table, columns):
    rows, width = slab.shape
    pw = pivots.shape[1]
    np_ = 2 * pw
    ncol = NXH * NZ
    place = lax.axis_index("col")
    z, xhi = place % NZ, place // NZ
    cols = place * width + jnp.arange(width, dtype=jnp.int32)
    home, goal, goes, dest_rank = table[2], table[3], table[4] > 0, table[5]
    hit = table[6, pw:] > 0
    dest = goal // width

    packed = pack(table, slab)
    sketch_part = sketch_sum(sketch_op, slab)
    other = col(packed, XH_SWAP)
    shard = packed + other
    shard, sketch_part = lax.optimization_barrier((shard, sketch_part))
    half = PAIR_CAP // 2 // 8 * 8
    up1 = col(shard, Z_UP)
    down1 = col(shard, Z_DOWN)
    chunk = rows // ncol
    leaving = leave(block_order, slab, ncol).reshape(NXH, NZ, np_, chunk)
    up1, down1, leaving = lax.optimization_barrier((up1, down1, leaving))
    up2, down2 = col(up1, Z_UP), col(down1, Z_DOWN)
    sketch_part = exchange_sum(sketch_part, "row")
    up3, down3 = col(up2, Z_UP), col(down2, Z_DOWN)
    up3, down3, sketch_part = lax.optimization_barrier((up3, down3, sketch_part))
    up4, down4 = col(up3[:half], Z_UP), col(down3[half:], Z_DOWN)
    sketch = spread_rows(sketch_part)

    shards = (shard, up1, up2, up3, up4, down4, down3, down2, down1)
    pivot_rows, sums_part = project(columns, slab, sketch_op, shards)
    leaving, sums_part = lax.optimization_barrier((leaving, sums_part))
    sums = exchange_sum(sums_part, "row")

    def for_z(step):
        return lax.dynamic_index_in_dim(leaving, (z + step) % NZ, 1, keepdims=False)

    far = for_z(4)
    goes_up = col(far[:, : np_ // 2], Z_UP)
    goes_down = col(far[:, np_ // 2 :], Z_DOWN)
    goes_up, goes_down = lax.optimization_barrier((goes_up, goes_down))

    gram, inverse = joint_factor(sums[:, :np_])
    by_goal = (
        ((dest * DEST_CAP + dest_rank)[None, :] == jnp.arange(ncol * DEST_CAP)[:, None])
        & goes[None, :]
    ).astype(F32)
    taken = (home[:, None] == cols[None, :]).astype(F32)
    pieces = jnp.concatenate([sums[:, 2 * np_ :], sketch_part], axis=0)
    small = pieces.shape[0] // 2
    sent = dot(by_goal, dot(taken, pieces, 1, 1), 1, 0)
    sent = sent.reshape(ncol, DEST_CAP, pieces.shape[0])
    sent = lax.all_to_all(sent, "col", 0, 0)
    new_sums = jnp.sum(sent, axis=0).T
    rest = jnp.concatenate([sums[:, np_:], new_sums[:small], new_sums[small:]], axis=1)
    rest = spread_rows(rest)
    pivot_sketch, product = rest[:, :np_], rest[:, np_ : np_ + width]
    late = rest[:, np_ + width :]
    new_product, new_sketch = late[:, :DEST_CAP], late[:, DEST_CAP:]

    zero = jnp.zeros_like(goes_up)
    goes_up = for_z(3) + jnp.concatenate([goes_up, zero], axis=1)
    goes_down = for_z(-3) + jnp.concatenate([zero, goes_down], axis=1)
    for step in (2, 1, 0):
        goes_up = col(goes_up, Z_UP)
        goes_down = col(goes_down, Z_DOWN)
        goes_up, goes_down = lax.optimization_barrier((goes_up, goes_down))
        if step > 0:
            goes_up, goes_down = for_z(step) + goes_up, for_z(-step) + goes_down
    arrived = for_z(0) + goes_up + goes_down
    keep = lax.dynamic_index_in_dim(arrived, xhi, 0, keepdims=False)
    give = lax.dynamic_index_in_dim(arrived, 1 - xhi, 0, keepdims=False)
    give = col(give, XH_SWAP)
    arrived = keep + give
    outgoing = dot(by_goal, arrived, 1, 0).reshape(ncol, DEST_CAP, chunk)
    incoming = lax.all_to_all(outgoing, "col", 0, 0)
    new_rows = jnp.swapaxes(incoming, 0, 1).reshape(DEST_CAP, rows)

    in0 = cols // pw == block_order[0]
    in1 = cols // pw == block_order[1]
    at = (goal[:, None] == cols[None, :]) & goes[:, None]
    is_new = jnp.any(at, axis=0)
    slot_of = jnp.sum(jnp.where(at, dest_rank[:, None], 0), axis=0)
    put_new = (jnp.arange(DEST_CAP)[:, None] == slot_of[None, :]) & is_new[None, :]
    which = jnp.arange(np_, dtype=jnp.int32)
    put_pivot = (home[:, None] == cols[None, :])
    at0 = at & (which < pw)[:, None]
    is_new0 = jnp.any(at0, axis=0)
    put_new0 = put_new & is_new0[None, :]
    met = (pivots[1][:, None] == cols[None, :]) & hit[:, None]
    put_pivot0 = jnp.concatenate([put_pivot[:pw], met], axis=0)
    is_old0 = ~(is_new0 | in0 | jnp.any(met, axis=0))
    is_old = ~(is_new | in0 | in1)

    first_source = jnp.concatenate([new_product, gram], axis=1)
    put = jnp.concatenate([put_new, put_pivot], axis=0).astype(F32)
    put0 = jnp.concatenate([put_new0, put_pivot0], axis=0).astype(F32)
    before = jnp.where(is_old0[None, :], product, 0.0) + dot(first_source, put0, 1, 0)
    after = jnp.where(is_old[None, :], product, 0.0) + dot(first_source, put, 1, 0)
    top = dot(inverse[:pw], before, 1, 0)
    solved = dot(inverse, after, 1, 0)
    done = in0 | in1
    low = jnp.where(in0[None, :], 0.0, solved[pw:])
    factors = jnp.concatenate([top, low], axis=0)
    weights = jnp.concatenate(
        [
            jnp.where(in0[None, :], 0.0, solved[:pw]),
            jnp.where(done[None, :], 0.0, solved[pw:]),
        ],
        axis=0,
    )
    weights = dot(inverse, weights, 0, 0)
    mix = put - jnp.concatenate([jnp.zeros((DEST_CAP, width), F32), weights], axis=0)
    both_rows = jnp.concatenate([new_rows, pivot_rows], axis=0)
    slab_out = jnp.where(is_old[None, :], slab, 0.0) + dot(both_rows, mix, 0, 0, lax.Precision.HIGH)
    both_sketch = jnp.concatenate([new_sketch, pivot_sketch], axis=1)
    sketch_out = jnp.where(is_old[None, :], sketch, 0.0) + dot(both_sketch, mix, 1, 0, lax.Precision.HIGH)
    sketch_out = jnp.where(done[None, :], 0.0, sketch_out)
    return slab_out, factors, sketch_out


def local(slab, sketch_op, block_order, pivots):
    table, columns, fits = plan(block_order, pivots)
    outs = joint(slab, sketch_op, block_order, pivots, table, columns)

    def again(carry):
        results = general(hold(slab), hold(sketch_op), block_order, pivots)
        return (jnp.ones_like(fits[0]), *(hold(x) for x in results))

    outs = lax.while_loop(lambda carry: carry[0] == 0, again, (fits[0], *outs))
    return outs[1:]


def solution(mesh):
    return jax.shard_map(
        local,
        mesh=mesh,
        in_specs=(P("row", "col"), P(None, "row"), P(), P()),
        out_specs=(P("row", "col"), P(None, "col"), P(None, "col")),
        check_vma=False,
    )
```

```python
import jax
import jax.numpy as jnp
from jax import lax
from jax.experimental import pallas as pl
from jax.experimental.pallas import tpu as pltpu
from jax.sharding import PartitionSpec as P


HI = lax.Precision.HIGHEST
F32 = jnp.float32

NX, NY, NCORE, NXH, NZ = 2, 4, 2, 2, 8
PAIR_CAP = 56
DEST_CAP = 32


def dot(a, b, ca, cb, precision=HI):
    return lax.dot_general(
        a, b, (((ca,), (cb,)), ((), ())), precision=precision, preferred_element_type=F32
    )


BLOCK = 128
SHIFT = 9
STRIP = 16
VM = pl.BlockSpec(memory_space=pltpu.VMEM)
BF16 = jnp.bfloat16


def split2(x):
    high = x.astype(BF16)
    return high, (x - high.astype(F32)).astype(BF16)


def split3(x):
    high, rest = x.astype(BF16), None
    left = x - high.astype(F32)
    middle = left.astype(BF16)
    rest = (left - middle.astype(F32)).astype(BF16)
    return high, middle, rest


def dot3(a, b, ca, cb):
    a0, a1 = a
    b0, b1 = b
    return (
        dot(a0, b1, ca, cb, None) + dot(a1, b0, ca, cb, None)
    ) + dot(a0, b0, ca, cb, None)


def dot6(a, b):
    terms = ((0, 2), (2, 0), (1, 1), (0, 1), (1, 0), (0, 0))
    return sum(dot(a[i], b[j], 1, 0, None) for i, j in terms)


def factor_block(s_ref, w_ref, n):
    sub = lax.broadcasted_iota(jnp.int32, (STRIP, n), 0)
    lane = lax.broadcasted_iota(jnp.int32, (STRIP, n), 1)
    w_ref[...] = (
        lax.broadcasted_iota(jnp.int32, (n, n), 0) == lax.broadcasted_iota(jnp.int32, (n, n), 1)
    ).astype(F32)

    @pl.loop(0, n // STRIP)
    def _(k):
        start = pl.multiple_of(k * STRIP, STRIP)
        v = s_ref[pl.ds(start, STRIP), :]
        w = w_ref[pl.ds(start, STRIP), :]
        turned = pltpu.roll(v, lax.rem(n - start, n), 1)
        lanes = [jnp.broadcast_to(turned[:, m : m + 1], (STRIP, n)) for m in range(STRIP)]
        scale = jnp.zeros((STRIP, n), F32)
        for i in range(STRIP):
            pivot = lanes[i][i : i + 1, :]
            scale = jnp.where(sub == i, pivot, scale)
            if i == STRIP - 1:
                break
            f = jnp.where(sub > i, lanes[i] * (1.0 / pivot), 0.0)
            for m in range(i + 1, STRIP):
                lanes[m] = lanes[m] - f * lanes[m][i : i + 1, :]
            v = v - f * v[i : i + 1, :]
            w = w - f * w[i : i + 1, :]
        root = 1.0 / jnp.sqrt(scale)
        v, w = v * root, w * root
        w_ref[pl.ds(start, STRIP), :] = w
        below = jnp.where(lane >= start + STRIP, v, 0.0)
        update = dot(below, jnp.concatenate([v, w], axis=1), 0, 0)
        s_ref[...] = s_ref[...] - update[:, :n]
        w_ref[...] = w_ref[...] - update[:, n:]


def inverse_factor_kernel(gram_ref, out_ref, s_ref, w_ref):
    n = s_ref.shape[0]
    s_ref[...] = gram_ref[:n, :n]
    factor_block(s_ref, w_ref, n)
    inv0 = w_ref[...]
    if gram_ref.shape[0] == n:
        out_ref[...] = inv0
        return
    cross = dot(gram_ref[n:, :n], inv0, 1, 1)
    out_ref[:n, :n] = inv0
    out_ref[:n, n:] = jnp.zeros((n, n), F32)
    s_ref[...] = gram_ref[n:, n:] - dot(cross, cross, 1, 1)
    lead = dot(cross, inv0, 1, 0)
    factor_block(s_ref, w_ref, n)
    inv1 = w_ref[...]
    out_ref[n:, :n] = -dot(inv1, lead, 1, 0)
    out_ref[n:, n:] = inv1


def joint_factor_kernel(near_ref, other_ref, gram_ref, out_ref, s_ref, w_ref):
    here = lax.axis_index("row")
    core = lax.rem(here, NCORE)
    y = lax.rem(here // NCORE, NY)
    x = here // (NCORE * NY)
    m = 16
    for c, ref in enumerate((near_ref, other_ref)):
        for t in range(NX):
            for i in range(NY):
                chunk = ((x ^ t) * NY + lax.rem(y + i, NY)) * NCORE + (core ^ c)
                at = (t * NY + i) * m
                gram_ref[pl.ds(pl.multiple_of(chunk * m, m), m), :] = ref[at : at + m, :]
    inverse_factor_kernel(gram_ref, out_ref, s_ref, w_ref)


def joint_factor(mine):
    half = mine.shape[0] // 2
    up = row(mine, Y_UP)
    down = row(mine, Y_DOWN)
    up, down = lax.optimization_barrier((up, down))
    far_top = row(up[:half], Y_UP)
    far_low = row(down[half:], Y_DOWN)
    ring = jnp.concatenate([mine, down, far_top, far_low, up], axis=0)
    near = jnp.concatenate([ring, row(ring, X_SWAP)], axis=0)
    other = row(near, CORE_SWAP)
    n = mine.shape[1]
    shape = jax.ShapeDtypeStruct((n, n), F32)
    return pl.pallas_call(
        joint_factor_kernel,
        out_shape=(shape, shape),
        in_specs=[VM, VM],
        out_specs=(VM, VM),
        scratch_shapes=[pltpu.VMEM((BLOCK, BLOCK), F32)] * 2,
        cost_estimate=pl.CostEstimate(
            flops=10_000_000_000, bytes_accessed=3 * n * n * 4, transcendentals=0
        ),
        name="joint_factor",
    )(near, other)


def inverse_factor(gram):
    n = gram.shape[0]
    return pl.pallas_call(
        inverse_factor_kernel,
        out_shape=jax.ShapeDtypeStruct((n, n), F32),
        in_specs=[VM],
        out_specs=VM,
        scratch_shapes=[pltpu.VMEM((BLOCK, BLOCK), F32)] * 2,
        cost_estimate=pl.CostEstimate(flops=20_000_000, bytes_accessed=2 * n * n * 4, transcendentals=0),
        name="inverse_factor",
    )(gram)


def plan_kernel(order_ref, pivots_ref, table_ref, columns_ref, fits_ref):
    place = lax.axis_index("col")
    z = lax.rem(place, NZ)
    pw, wide = BLOCK, 2 * BLOCK
    pivots = pivots_ref[...]
    pivot_cols = jnp.concatenate([pivots.astype(F32), jnp.zeros((pw - 2, pw), F32)], axis=0)
    pivot_cols = pivot_cols.T.astype(jnp.int32)
    first, second = pivots[0:1, :], pivots[1:2, :]
    sub = lax.broadcasted_iota(jnp.int32, (pw, pw), 0)
    lane = lax.broadcasted_iota(jnp.int32, (1, pw), 1)
    meet = pivot_cols[:, 0:1] == second
    met_by = pivot_cols[:, 1:2] == first
    hit = jnp.sum(meet.astype(jnp.int32), axis=0, keepdims=True)
    lost = jnp.sum(met_by.astype(jnp.int32), axis=0, keepdims=True)
    start0, start1 = order_ref[0] * pw, order_ref[1] * pw
    moved = start0 + jnp.sum(jnp.where(meet, sub, 0), axis=0, keepdims=True)
    source = jnp.concatenate([first, jnp.where(hit > 0, moved, second)], axis=1)
    home = jnp.concatenate([start0 + lane, start1 + lane], axis=1)
    goal = jnp.concatenate([first, second], axis=1)
    goes = jnp.concatenate([1 - lost, jnp.ones_like(lost)], axis=1)
    met = jnp.concatenate([jnp.zeros_like(hit), hit], axis=1)
    pair = (source >> SHIFT) & (NZ - 1)
    dest = jnp.where(goes > 0, goal >> SHIFT, -1)
    ends = jnp.where(goes > 0, dest & (NZ - 1), -1)
    blank = jnp.zeros((pw - 3, wide), F32)
    groups = jnp.concatenate(
        [pair.astype(F32), dest.astype(F32), ends.astype(F32), blank], axis=0
    ).T
    groups = groups.astype(jnp.int32)
    earlier = lax.broadcasted_iota(jnp.int32, (wide, wide), 0) < lax.broadcasted_iota(
        jnp.int32, (wide, wide), 1
    )
    pair_rank = jnp.sum(
        ((groups[:, 0:1] == pair) & earlier).astype(jnp.int32), axis=0, keepdims=True
    )
    dest_rank = jnp.sum(
        ((groups[:, 1:2] == dest) & earlier).astype(jnp.int32), axis=0, keepdims=True
    )
    ends_rank = jnp.sum(
        ((groups[:, 2:3] == ends) & earlier).astype(jnp.int32), axis=0, keepdims=True
    )
    slot = ((z - pair) & (NZ - 1)) * PAIR_CAP + pair_rank
    table = jnp.concatenate(
        [source, pair_rank, home, goal, goes, dest_rank, met, slot, ends, ends_rank]
        + [jnp.zeros_like(slot)] * 6,
        axis=0,
    )
    table_ref[...] = table
    rows = jnp.concatenate([table.astype(F32), jnp.zeros((pw - 16, wide), F32)], axis=0)
    columns_ref[...] = rows.T.astype(jnp.int32)
    most = jnp.maximum(
        jnp.max(pair_rank) - PAIR_CAP, jnp.max(jnp.where(goes > 0, dest_rank, 0)) - DEST_CAP
    )
    most = jnp.maximum(most, jnp.max(jnp.where(goes > 0, ends_rank, 0)) - PAIR_CAP)
    fits_ref[0] = (most < 0).astype(jnp.int32)


def plan(block_order, pivots):
    wide = 2 * BLOCK
    smem = pl.BlockSpec(memory_space=pltpu.SMEM)
    shape = jax.ShapeDtypeStruct
    return pl.pallas_call(
        plan_kernel,
        out_shape=(
            shape((16, wide), jnp.int32),
            shape((wide, BLOCK), jnp.int32),
            shape((1,), jnp.int32),
        ),
        in_specs=[smem, VM],
        out_specs=(VM, VM, smem),
        name="plan",
    )(block_order, pivots)


def pack_kernel(table_ref, slab_ref, out_ref):
    slots, width = out_ref.shape[0], slab_ref.shape[1]
    place = lax.axis_index("col")
    source, rank = table_ref[0:1, :], table_ref[1:2, :]
    slot = lax.broadcasted_iota(jnp.int32, (slots, source.shape[1]), 0)
    mine = (rank == slot) & ((source >> SHIFT) == place)
    at = jnp.sum(jnp.where(mine, source - place * width + 1, 0), axis=1, keepdims=True) - 1
    take = (at == lax.broadcasted_iota(jnp.int32, (slots, width), 1)).astype(F32).astype(BF16)
    pieces = split3(slab_ref[...])
    out_ref[...] = sum(dot(take, p, 1, 1, None) for p in pieces[::-1])


def pack(table, slab):
    (rows, width), step = slab.shape, 512
    return pl.pallas_call(
        pack_kernel,
        out_shape=jax.ShapeDtypeStruct((PAIR_CAP, rows), F32),
        grid=(rows // step,),
        in_specs=[VM, pl.BlockSpec((step, width), lambda k: (k, 0))],
        out_specs=pl.BlockSpec((PAIR_CAP, step), lambda k: (0, k)),
        cost_estimate=pl.CostEstimate(
            flops=6 * PAIR_CAP * slab.size, bytes_accessed=8 * slab.size, transcendentals=0
        ),
        name="pack",
    )(table, slab)


def leave_kernel(order_ref, table_ref, slab_ref, out_ref):
    place = lax.axis_index("col")
    slots, width = out_ref.shape[0], slab_ref.shape[1]
    owned = [(order_ref[k] * BLOCK) >> SHIFT == place for k in range(2)]

    @pl.when(jnp.logical_or(owned[0], owned[1]))
    def _():
        home, goes, ends, rank = (table_ref[k : k + 1, :] for k in (2, 4, 8, 9))
        slot = lax.broadcasted_iota(jnp.int32, (slots, home.shape[1]), 0)
        mine = (ends * PAIR_CAP + rank == slot) & (goes > 0) & ((home >> SHIFT) == place)
        at = jnp.sum(jnp.where(mine, home - place * width + 1, 0), axis=1, keepdims=True) - 1
        here = lax.broadcasted_iota(jnp.int32, (slots, width), 1)
        take = (at == here).astype(F32).astype(BF16)
        pieces = split3(slab_ref[...])
        out_ref[...] = sum(dot(take, p, 1, 1, None) for p in pieces[::-1])

    @pl.when(jnp.logical_not(jnp.logical_or(owned[0], owned[1])))
    def _():
        out_ref[...] = jnp.zeros(out_ref.shape, F32)


def leave(order, table, slab):
    (rows, width), step, slots = slab.shape, 512, NZ * PAIR_CAP
    return pl.pallas_call(
        leave_kernel,
        out_shape=jax.ShapeDtypeStruct((slots, rows), F32),
        grid=(rows // step,),
        in_specs=[
            pl.BlockSpec(memory_space=pltpu.SMEM),
            VM,
            pl.BlockSpec((step, width), lambda k: (k, 0)),
        ],
        out_specs=pl.BlockSpec((slots, step), lambda k: (0, k)),
        cost_estimate=pl.CostEstimate(
            flops=slab.size, bytes_accessed=8 * slab.size, transcendentals=0
        ),
        name="leave",
    )(order, table, slab)


def project_kernel(columns_ref, slab_ref, op_ref, *refs):
    *shards, rows_ref, sums_ref, all_ref = refs
    count, total = columns_ref.shape[0], all_ref.shape[0]
    start = 0
    for shard in shards:
        all_ref[start : start + shard.shape[0], :] = shard[...]
        start += shard.shape[0]
    spread = (
        columns_ref[:, 7:8] == lax.broadcasted_iota(jnp.int32, (count, total), 1)
    ).astype(F32).astype(BF16)

    @pl.when(pl.program_id(0) == 0)
    def _():
        sums_ref[...] = jnp.zeros(sums_ref.shape, F32)

    pieces = split3(all_ref[...])
    pivot = sum(dot(spread, p, 1, 0, None) for p in pieces[::-1])
    rows_ref[...] = pivot
    three = split3(pivot)
    turned = [p.T for p in three]
    sums_ref[:, :count] += dot6(three, turned)
    sums_ref[:, count : 2 * count] += dot3(split2(op_ref[...]), turned[:2], 1, 0)
    sums_ref[:, 2 * count :] += dot3(three[:2], split2(slab_ref[...]), 1, 0)


def project(columns, slab, sketch_op, shards):
    count, (rows, width), step = columns.shape[0], slab.shape, 512
    total = sum(s.shape[0] for s in shards)
    across = lambda n: pl.BlockSpec((n, step), lambda k: (0, k))
    shape = jax.ShapeDtypeStruct
    return pl.pallas_call(
        project_kernel,
        out_shape=(
            shape((count, rows), F32),
            shape((count, 2 * count + width), F32),
        ),
        grid=(rows // step,),
        in_specs=[
            VM,
            pl.BlockSpec((step, width), lambda k: (k, 0)),
            across(sketch_op.shape[0]),
            *(across(s.shape[0]) for s in shards),
        ],
        out_specs=(
            across(count),
            pl.BlockSpec((count, 2 * count + width), lambda k: (0, 0)),
        ),
        scratch_shapes=[pltpu.VMEM((total, step), F32)],
        cost_estimate=pl.CostEstimate(
            flops=6 * count * rows * (total + 2 * count + width),
            bytes_accessed=4 * (slab.size + sketch_op.size + total * rows + count * rows),
            transcendentals=0,
        ),
        name="project",
    )(columns, slab, sketch_op, *shards)


def one_hot_dot(a, b):
    return sum(dot(p, b.astype(F32).astype(BF16), 1, 0, None) for p in split3(a)[::-1])


def weigh_kernel(order_ref, columns_ref, gram_ref, inv_ref, rest_ref, sketch_ref, *outs):
    factors_ref, mix_ref, new_ref, keep_ref, sketch_out_ref = outs
    place = lax.axis_index("col")
    count, width = gram_ref.shape[0], sketch_ref.shape[1]
    pw = BLOCK
    cols = place * width + lax.broadcasted_iota(jnp.int32, (1, width), 1)
    home, goal, goes, dest_rank, met, ends_rank = (
        columns_ref[:, k : k + 1] for k in (2, 3, 4, 5, 6, 9)
    )

    def any_row(mask):
        return jnp.max(mask.astype(jnp.int32), axis=0, keepdims=True) > 0

    def spot(mask, rank, cap):
        slot = jnp.sum(jnp.where(mask, rank + 1, 0), axis=0, keepdims=True) - 1
        return lax.broadcasted_iota(jnp.int32, (cap, width), 0) == slot

    at = (goal == cols) & (goes > 0)
    is_new, is_new0 = any_row(at), any_row(at[:pw])
    put_new, put_new0 = spot(at, dest_rank, DEST_CAP), spot(at[:pw], dest_rank[:pw], DEST_CAP)
    put = home == cols
    again = ((goal == cols) & (met > 0))[pw:]
    put0 = jnp.concatenate([put[:pw].astype(F32), again.astype(F32)], axis=0)
    put = put.astype(F32)
    in0, in1 = cols >> 7 == order_ref[0], cols >> 7 == order_ref[1]
    is_old0 = jnp.logical_not(is_new0 | in0 | any_row(again))
    is_old = jnp.logical_not(is_new | in0 | in1)
    gram = gram_ref[...]
    pivot_sketch, product = rest_ref[:, :count], rest_ref[:, count : count + width]
    late = rest_ref[:, count + width :]
    new_product, new_sketch = late[:, :DEST_CAP], late[:, DEST_CAP:]
    before = jnp.where(is_old0, product, 0.0) + one_hot_dot(gram, put0)
    before += one_hot_dot(new_product, put_new0)
    after = jnp.where(is_old, product, 0.0) + one_hot_dot(gram, put)
    after += one_hot_dot(new_product, put_new)
    inverse = inv_ref[...]
    factors_ref[:pw, :] = dot(inverse[:pw], before, 1, 0)
    solved = dot(inverse, after, 1, 0)
    factors_ref[pw:, :] = jnp.where(in0, 0.0, solved[pw:])
    weights = jnp.concatenate(
        [jnp.where(in0, 0.0, solved[:pw]), jnp.where(in0 | in1, 0.0, solved[pw:])], axis=0
    )
    mix = put - dot(inverse, weights, 0, 0)
    mix_ref[...] = mix
    new_ref[...] = spot(at, ends_rank, new_ref.shape[0]).astype(F32)
    keep_ref[...] = is_old.astype(F32)
    sketch = jnp.where(is_old, sketch_ref[...], 0.0) + one_hot_dot(new_sketch, put_new)
    sketch += dot3(split2(pivot_sketch), split2(mix), 1, 0)
    sketch_out_ref[...] = jnp.where(in0 | in1, 0.0, sketch)


def weigh(order, columns, gram, inverse, rest, sketch):
    count, width = gram.shape[0], sketch.shape[1]
    shape = lambda n: jax.ShapeDtypeStruct((n, width), F32)
    return pl.pallas_call(
        weigh_kernel,
        out_shape=(shape(count), shape(count), shape(64), shape(1), shape(count)),
        in_specs=[pl.BlockSpec(memory_space=pltpu.SMEM)] + [VM] * 5,
        out_specs=(VM,) * 5,
        cost_estimate=pl.CostEstimate(
            flops=60 * count * count * width, bytes_accessed=20 * count * width, transcendentals=0
        ),
        name="weigh",
    )(order, columns, gram, inverse, rest, sketch)


def finish_kernel(slab_ref, rows_ref, own_ref, other_ref, mix_ref, new_ref, keep_ref, out_ref):
    arrived = own_ref[...] + other_ref[...]
    blank = jnp.zeros((new_ref.shape[0] - arrived.shape[0], arrived.shape[1]), F32)
    arrived = jnp.concatenate([arrived, blank], axis=0)
    pieces = split3(arrived)[::-1]
    put = new_ref[...].astype(BF16)
    total = dot3(split2(rows_ref[...]), split2(mix_ref[...]), 0, 0)
    total += sum(dot(p, put, 0, 0, None) for p in pieces)
    out_ref[...] = jnp.where(keep_ref[...] > 0.0, slab_ref[...], 0.0) + total


def finish(slab, pivot_rows, own, other, mix, new, keep):
    (rows, width), step = slab.shape, 512
    across = lambda n: pl.BlockSpec((n, step), lambda k: (0, k))
    block = pl.BlockSpec((step, width), lambda k: (k, 0))
    return pl.pallas_call(
        finish_kernel,
        out_shape=jax.ShapeDtypeStruct(slab.shape, F32),
        grid=(rows // step,),
        in_specs=[
            block,
            across(pivot_rows.shape[0]),
            across(own.shape[0]),
            across(other.shape[0]),
            VM,
            VM,
            VM,
        ],
        out_specs=block,
        cost_estimate=pl.CostEstimate(
            flops=6 * pivot_rows.size * width, bytes_accessed=8 * slab.size, transcendentals=0
        ),
        name="finish",
    )(slab, pivot_rows, own, other, mix, new, keep)


def sketch_kernel(op_ref, slab_ref, out_ref):
    @pl.when(pl.program_id(0) == 0)
    def _():
        out_ref[...] = jnp.zeros(out_ref.shape, F32)

    out_ref[...] += dot3(split2(op_ref[...]), split2(slab_ref[...]), 1, 0)


def sketch_sum(sketch_op, slab):
    count, (rows, width), step = sketch_op.shape[0], slab.shape, 512
    return pl.pallas_call(
        sketch_kernel,
        out_shape=jax.ShapeDtypeStruct((count, width), F32),
        grid=(rows // step,),
        in_specs=[
            pl.BlockSpec((count, step), lambda k: (0, k)),
            pl.BlockSpec((step, width), lambda k: (k, 0)),
        ],
        out_specs=pl.BlockSpec((count, width), lambda k: (0, 0)),
        cost_estimate=pl.CostEstimate(
            flops=6 * count * slab.size,
            bytes_accessed=4 * (slab.size + sketch_op.size),
            transcendentals=0,
        ),
        name="sketch_sum",
    )(sketch_op, slab)


def row_perm(f):
    out = []
    for x in range(NX):
        for y in range(NY):
            for c in range(NCORE):
                u, v, w = f(x, y, c)
                out.append(((x * NY + y) * NCORE + c, (u * NY + v % NY) * NCORE + w))
    return out


def col_perm(f):
    out = []
    for x in range(NXH):
        for z in range(NZ):
            u, v = f(x, z)
            out.append((x * NZ + z, u * NZ + v % NZ))
    return out


Y_UP = row_perm(lambda x, y, c: (x, y + 1, c))
Y_DOWN = row_perm(lambda x, y, c: (x, y - 1, c))
X_SWAP = row_perm(lambda x, y, c: (1 - x, y, c))
CORE_SWAP = row_perm(lambda x, y, c: (x, y, 1 - c))
Z_UP = col_perm(lambda x, z: (x, z + 1))
Z_DOWN = col_perm(lambda x, z: (x, z - 1))
XH_SWAP = col_perm(lambda x, z: (1 - x, z))


def row(x, perm):
    return lax.ppermute(x, "row", perm)


def col(x, perm):
    return lax.ppermute(x, "col", perm)


def hold_kernel(in_ref, out_ref):
    out_ref[...] = in_ref[...]


def hold(x):
    block = pl.BlockSpec((128, 512), lambda i, j: (i, j))
    return pl.pallas_call(
        hold_kernel,
        out_shape=jax.ShapeDtypeStruct(x.shape, x.dtype),
        grid=(x.shape[0] // 128, x.shape[1] // 512),
        in_specs=[block],
        out_specs=block,
        name="hold",
    )(x)


def exchange_sum(x, axis):
    n = lax.axis_size(axis)
    parts = x.reshape(n, x.shape[0] // n, *x.shape[1:])
    return jnp.sum(lax.all_to_all(parts, axis, 0, 0), axis=0)


def all_sum(x, axis):
    n = lax.axis_size(axis)
    mine = exchange_sum(x, axis)
    spread = jnp.broadcast_to(mine[None], (n, *mine.shape))
    return lax.all_to_all(spread, axis, 0, 0).reshape(x.shape)


def spread_rows(x):
    n = lax.axis_size("row")
    copies = jnp.broadcast_to(x[None], (n, *x.shape))
    return lax.all_to_all(copies, "row", 0, 0).reshape(n * x.shape[0], x.shape[1])


def general(slab, sketch_op, block_order, pivots):
    width, pw = slab.shape[1], pivots.shape[1]
    place = lax.axis_index("col")
    base = place * width
    cols = base + jnp.arange(width, dtype=jnp.int32)
    sketch = all_sum(dot(sketch_op, slab, 1, 0), "row")

    def panel(k, carry):
        slab, sketch, finished, factors = carry
        start = block_order[k] * pw
        owner = start // width
        offset = start - owner * width
        owns = place == owner
        local = pivots[k] - base
        selector = (jnp.arange(width)[:, None] == local[None, :]).astype(F32)
        targeted = jnp.sum(selector, axis=1) > 0.5
        both = jnp.concatenate([slab, sketch])
        block = lax.dynamic_slice_in_dim(both, offset, pw, 1)
        moved = jnp.concatenate(
            [dot(both, selector, 1, 0), jnp.where(owns, block, 0.0)], axis=1
        )
        moved = all_sum(moved, "col")
        panel_cols, displaced = moved[:, :pw], moved[:, pw:]
        both = lax.dynamic_update_slice_in_dim(
            both, jnp.where(owns, panel_cols, block), offset, 1
        )
        both = jnp.where(targeted[None, :], dot(displaced, selector, 1, 1), both)
        slab, sketch = both[: slab.shape[0]], both[slab.shape[0] :]
        panel_slab, panel_sketch = panel_cols[: slab.shape[0]], panel_cols[slab.shape[0] :]
        gram = all_sum(dot(panel_slab, panel_slab, 0, 0), "row")
        inverse = inverse_factor(gram)
        basis = dot(panel_slab, inverse, 1, 1)
        projected = all_sum(dot(basis, slab, 0, 0), "row")
        factors = lax.dynamic_update_slice_in_dim(
            factors, jnp.where(finished[None, :], 0.0, projected), k * pw, 0
        )
        finished = finished | (cols // pw == block_order[k])
        slab = jnp.where(finished[None, :], slab, slab - dot(basis, projected, 1, 0))
        update = dot(dot(panel_sketch, inverse, 1, 1), projected, 1, 0)
        sketch = jnp.where(finished[None, :], 0.0, sketch - update)
        return slab, sketch, finished, factors

    carry = (
        slab,
        sketch,
        jnp.zeros((width,), dtype=bool),
        jnp.zeros((pivots.shape[0] * pw, width), F32),
    )
    slab, sketch, _, factors = lax.fori_loop(0, pivots.shape[0], panel, carry)
    return slab, factors, sketch


def joint(slab, sketch_op, block_order, pivots, table, columns):
    rows, width = slab.shape
    pw = pivots.shape[1]
    np_ = 2 * pw
    ncol = NXH * NZ
    place = lax.axis_index("col")
    z = place % NZ
    cols = place * width + jnp.arange(width, dtype=jnp.int32)
    home, goal, goes, dest_rank = table[2], table[3], table[4] > 0, table[5]
    dest = goal // width

    packed = pack(table, slab)
    sketch_part = sketch_sum(sketch_op, slab)
    other = col(packed, XH_SWAP)
    shard = packed + other
    shard, sketch_part = lax.optimization_barrier((shard, sketch_part))
    half = PAIR_CAP // 2 // 8 * 8
    up1 = col(shard, Z_UP)
    down1 = col(shard, Z_DOWN)
    leaving = leave(block_order, table, slab).reshape(NZ, PAIR_CAP, rows)
    up1, down1, leaving = lax.optimization_barrier((up1, down1, leaving))
    up2, down2 = col(up1, Z_UP), col(down1, Z_DOWN)
    sketch_part = exchange_sum(sketch_part, "row")
    up3, down3 = col(up2, Z_UP), col(down2, Z_DOWN)
    up3, down3, sketch_part = lax.optimization_barrier((up3, down3, sketch_part))
    up4, down4 = col(up3[:half], Z_UP), col(down3[half:], Z_DOWN)
    sketch = spread_rows(sketch_part)

    shards = (shard, up1, up2, up3, up4, down4, down3, down2, down1)
    pivot_rows, sums_part = project(columns, slab, sketch_op, shards)
    leaving, sums_part = lax.optimization_barrier((leaving, sums_part))
    sums = exchange_sum(sums_part, "row")

    def for_z(step):
        return lax.dynamic_index_in_dim(leaving, (z + step) % NZ, 0, keepdims=False)

    far = for_z(4)
    goes_up = col(far[:half], Z_UP)
    goes_down = col(far[half:], Z_DOWN)
    goes_up, goes_down = lax.optimization_barrier((goes_up, goes_down))

    gram, inverse = joint_factor(sums[:, :np_])
    by_goal = (
        ((dest * DEST_CAP + dest_rank)[None, :] == jnp.arange(ncol * DEST_CAP)[:, None])
        & goes[None, :]
    ).astype(F32)
    taken = (home[:, None] == cols[None, :]).astype(F32)
    pieces = jnp.concatenate([sums[:, 2 * np_ :], sketch_part], axis=0)
    small = pieces.shape[0] // 2
    sent = dot(by_goal, dot(taken, pieces, 1, 1), 1, 0)
    sent = sent.reshape(ncol, DEST_CAP, pieces.shape[0])
    sent = lax.all_to_all(sent, "col", 0, 0)
    new_sums = jnp.sum(sent, axis=0).T
    rest = jnp.concatenate([sums[:, np_:], new_sums[:small], new_sums[small:]], axis=1)
    rest = spread_rows(rest)

    goes_up = for_z(3) + jnp.pad(goes_up, ((0, PAIR_CAP - half), (0, 0)))
    goes_down = for_z(-3) + jnp.pad(goes_down, ((half, 0), (0, 0)))
    for step in (2, 1, 0):
        goes_up = col(goes_up, Z_UP)
        goes_down = col(goes_down, Z_DOWN)
        goes_up, goes_down = lax.optimization_barrier((goes_up, goes_down))
        if step > 0:
            goes_up, goes_down = for_z(step) + goes_up, for_z(-step) + goes_down
    arrived = for_z(0) + goes_up + goes_down
    other = col(arrived, XH_SWAP)
    factors, mix, new, keep, sketch_out = weigh(block_order, columns, gram, inverse, rest, sketch)
    return finish(slab, pivot_rows, arrived, other, mix, new, keep), factors, sketch_out


def local(slab, sketch_op, block_order, pivots):
    table, columns, fits = plan(block_order, pivots)
    outs = joint(slab, sketch_op, block_order, pivots, table, columns)

    def again(carry):
        results = general(hold(slab), hold(sketch_op), block_order, pivots)
        return (jnp.ones_like(fits[0]), *(hold(x) for x in results))

    outs = lax.while_loop(lambda carry: carry[0] == 0, again, (fits[0], *outs))
    return outs[1:]


def solution(mesh):
    return jax.shard_map(
        local,
        mesh=mesh,
        in_specs=(P("row", "col"), P(None, "row"), P(), P()),
        out_specs=(P("row", "col"), P(None, "col"), P(None, "col")),
        check_vma=False,
    )
```

```python
import jax
import jax.numpy as jnp
from jax import lax
from jax.experimental import pallas as pl
from jax.experimental.pallas import tpu as pltpu
from jax.sharding import PartitionSpec as P


HI = lax.Precision.HIGHEST
F32 = jnp.float32

NX, NY, NCORE, NXH, NZ = 2, 4, 2, 2, 8
PAIR_CAP = 56
DEST_CAP = 32


def dot(a, b, ca, cb, precision=HI):
    return lax.dot_general(
        a, b, (((ca,), (cb,)), ((), ())), precision=precision, preferred_element_type=F32
    )


BLOCK = 128
SHIFT = 9
STRIP = 16
VM = pl.BlockSpec(memory_space=pltpu.VMEM)
BF16 = jnp.bfloat16


def split2(x):
    high = x.astype(BF16)
    return high, (x - high.astype(F32)).astype(BF16)


def split3(x):
    high, rest = x.astype(BF16), None
    left = x - high.astype(F32)
    middle = left.astype(BF16)
    rest = (left - middle.astype(F32)).astype(BF16)
    return high, middle, rest


def dot3(a, b, ca, cb):
    a0, a1 = a
    b0, b1 = b
    return (
        dot(a0, b1, ca, cb, None) + dot(a1, b0, ca, cb, None)
    ) + dot(a0, b0, ca, cb, None)


def dot6(a, b):
    terms = ((0, 2), (2, 0), (1, 1), (0, 1), (1, 0), (0, 0))
    return sum(dot(a[i], b[j], 1, 0, None) for i, j in terms)


def factor_block(s_ref, w_ref, n):
    sub = lax.broadcasted_iota(jnp.int32, (STRIP, n), 0)
    lane = lax.broadcasted_iota(jnp.int32, (STRIP, n), 1)
    w_ref[...] = (
        lax.broadcasted_iota(jnp.int32, (n, n), 0) == lax.broadcasted_iota(jnp.int32, (n, n), 1)
    ).astype(F32)

    @pl.loop(0, n // STRIP)
    def _(k):
        start = pl.multiple_of(k * STRIP, STRIP)
        v = s_ref[pl.ds(start, STRIP), :]
        w = w_ref[pl.ds(start, STRIP), :]
        turned = pltpu.roll(v, lax.rem(n - start, n), 1)
        lanes = [jnp.broadcast_to(turned[:, m : m + 1], (STRIP, n)) for m in range(STRIP)]
        scale = jnp.zeros((STRIP, n), F32)
        for i in range(STRIP):
            pivot = lanes[i][i : i + 1, :]
            scale = jnp.where(sub == i, pivot, scale)
            if i == STRIP - 1:
                break
            f = jnp.where(sub > i, lanes[i] * (1.0 / pivot), 0.0)
            for m in range(i + 1, STRIP):
                lanes[m] = lanes[m] - f * lanes[m][i : i + 1, :]
            v = v - f * v[i : i + 1, :]
            w = w - f * w[i : i + 1, :]
        root = 1.0 / jnp.sqrt(scale)
        v, w = v * root, w * root
        w_ref[pl.ds(start, STRIP), :] = w
        below = jnp.where(lane >= start + STRIP, v, 0.0)
        update = dot(below, jnp.concatenate([v, w], axis=1), 0, 0)
        s_ref[...] = s_ref[...] - update[:, :n]
        w_ref[...] = w_ref[...] - update[:, n:]


def inverse_factor_kernel(gram_ref, out_ref, s_ref, w_ref):
    n = s_ref.shape[0]
    s_ref[...] = gram_ref[:n, :n]
    factor_block(s_ref, w_ref, n)
    inv0 = w_ref[...]
    if gram_ref.shape[0] == n:
        out_ref[...] = inv0
        return
    cross = dot(gram_ref[n:, :n], inv0, 1, 1)
    out_ref[:n, :n] = inv0
    out_ref[:n, n:] = jnp.zeros((n, n), F32)
    s_ref[...] = gram_ref[n:, n:] - dot(cross, cross, 1, 1)
    lead = dot(cross, inv0, 1, 0)
    factor_block(s_ref, w_ref, n)
    inv1 = w_ref[...]
    out_ref[n:, :n] = -dot(inv1, lead, 1, 0)
    out_ref[n:, n:] = inv1


def joint_factor_kernel(near_ref, other_ref, gram_ref, out_ref, s_ref, w_ref):
    here = lax.axis_index("row")
    core = lax.rem(here, NCORE)
    y = lax.rem(here // NCORE, NY)
    x = here // (NCORE * NY)
    m = 16
    for c, ref in enumerate((near_ref, other_ref)):
        for t in range(NX):
            for i in range(NY):
                chunk = ((x ^ t) * NY + lax.rem(y + i, NY)) * NCORE + (core ^ c)
                at = (t * NY + i) * m
                gram_ref[pl.ds(pl.multiple_of(chunk * m, m), m), :] = ref[at : at + m, :]
    inverse_factor_kernel(gram_ref, out_ref, s_ref, w_ref)


def joint_factor(mine):
    half = mine.shape[0] // 2
    up = row(mine, Y_UP)
    down = row(mine, Y_DOWN)
    up, down = lax.optimization_barrier((up, down))
    far_top = row(up[:half], Y_UP)
    far_low = row(down[half:], Y_DOWN)
    ring = jnp.concatenate([mine, down, far_top, far_low, up], axis=0)
    far = row(ring, X_SWAP)
    near = jnp.concatenate([ring, far], axis=0)
    other = row(near, CORE_SWAP)
    n = mine.shape[1]
    shape = jax.ShapeDtypeStruct((n, n), F32)
    return pl.pallas_call(
        joint_factor_kernel,
        out_shape=(shape, shape),
        in_specs=[VM, VM],
        out_specs=(VM, VM),
        scratch_shapes=[pltpu.VMEM((BLOCK, BLOCK), F32)] * 2,
        cost_estimate=pl.CostEstimate(
            flops=10_000_000_000, bytes_accessed=3 * n * n * 4, transcendentals=0
        ),
        name="joint_factor",
    )(near, other)


def inverse_factor(gram):
    n = gram.shape[0]
    return pl.pallas_call(
        inverse_factor_kernel,
        out_shape=jax.ShapeDtypeStruct((n, n), F32),
        in_specs=[VM],
        out_specs=VM,
        scratch_shapes=[pltpu.VMEM((BLOCK, BLOCK), F32)] * 2,
        cost_estimate=pl.CostEstimate(flops=20_000_000, bytes_accessed=2 * n * n * 4, transcendentals=0),
        name="inverse_factor",
    )(gram)


def plan_kernel(order_ref, pivots_ref, table_ref, columns_ref, fits_ref):
    place = lax.axis_index("col")
    z = lax.rem(place, NZ)
    pw, wide = BLOCK, 2 * BLOCK
    pivots = pivots_ref[...]
    pivot_cols = jnp.concatenate([pivots.astype(F32), jnp.zeros((pw - 2, pw), F32)], axis=0)
    pivot_cols = pivot_cols.T.astype(jnp.int32)
    first, second = pivots[0:1, :], pivots[1:2, :]
    sub = lax.broadcasted_iota(jnp.int32, (pw, pw), 0)
    lane = lax.broadcasted_iota(jnp.int32, (1, pw), 1)
    meet = pivot_cols[:, 0:1] == second
    met_by = pivot_cols[:, 1:2] == first
    hit = jnp.sum(meet.astype(jnp.int32), axis=0, keepdims=True)
    lost = jnp.sum(met_by.astype(jnp.int32), axis=0, keepdims=True)
    start0, start1 = order_ref[0] * pw, order_ref[1] * pw
    moved = start0 + jnp.sum(jnp.where(meet, sub, 0), axis=0, keepdims=True)
    source = jnp.concatenate([first, jnp.where(hit > 0, moved, second)], axis=1)
    home = jnp.concatenate([start0 + lane, start1 + lane], axis=1)
    goal = jnp.concatenate([first, second], axis=1)
    goes = jnp.concatenate([1 - lost, jnp.ones_like(lost)], axis=1)
    met = jnp.concatenate([jnp.zeros_like(hit), hit], axis=1)
    pair = (source >> SHIFT) & (NZ - 1)
    dest = jnp.where(goes > 0, goal >> SHIFT, -1)
    ends = jnp.where(goes > 0, dest & (NZ - 1), -1)
    blank = jnp.zeros((pw - 3, wide), F32)
    groups = jnp.concatenate(
        [pair.astype(F32), dest.astype(F32), ends.astype(F32), blank], axis=0
    ).T
    groups = groups.astype(jnp.int32)
    earlier = lax.broadcasted_iota(jnp.int32, (wide, wide), 0) < lax.broadcasted_iota(
        jnp.int32, (wide, wide), 1
    )
    pair_rank = jnp.sum(
        ((groups[:, 0:1] == pair) & earlier).astype(jnp.int32), axis=0, keepdims=True
    )
    dest_rank = jnp.sum(
        ((groups[:, 1:2] == dest) & earlier).astype(jnp.int32), axis=0, keepdims=True
    )
    ends_rank = jnp.sum(
        ((groups[:, 2:3] == ends) & earlier).astype(jnp.int32), axis=0, keepdims=True
    )
    slot = ((z - pair) & (NZ - 1)) * PAIR_CAP + pair_rank
    table = jnp.concatenate(
        [source, pair_rank, home, goal, goes, dest_rank, met, slot, ends, ends_rank]
        + [jnp.zeros_like(slot)] * 6,
        axis=0,
    )
    table_ref[...] = table
    rows = jnp.concatenate([table.astype(F32), jnp.zeros((pw - 16, wide), F32)], axis=0)
    columns_ref[...] = rows.T.astype(jnp.int32)
    most = jnp.maximum(
        jnp.max(pair_rank) - PAIR_CAP, jnp.max(jnp.where(goes > 0, dest_rank, 0)) - DEST_CAP
    )
    most = jnp.maximum(most, jnp.max(jnp.where(goes > 0, ends_rank, 0)) - PAIR_CAP)
    fits_ref[0] = (most < 0).astype(jnp.int32)


def plan(block_order, pivots):
    wide = 2 * BLOCK
    smem = pl.BlockSpec(memory_space=pltpu.SMEM)
    shape = jax.ShapeDtypeStruct
    return pl.pallas_call(
        plan_kernel,
        out_shape=(
            shape((16, wide), jnp.int32),
            shape((wide, BLOCK), jnp.int32),
            shape((1,), jnp.int32),
        ),
        in_specs=[smem, VM],
        out_specs=(VM, VM, smem),
        name="plan",
    )(block_order, pivots)


def pack_kernel(table_ref, slab_ref, out_ref):
    slots, width = out_ref.shape[0], slab_ref.shape[1]
    place = lax.axis_index("col")
    source, rank = table_ref[0:1, :], table_ref[1:2, :]
    slot = lax.broadcasted_iota(jnp.int32, (slots, source.shape[1]), 0)
    mine = (rank == slot) & ((source >> SHIFT) == place)
    at = jnp.sum(jnp.where(mine, source - place * width + 1, 0), axis=1, keepdims=True) - 1
    take = (at == lax.broadcasted_iota(jnp.int32, (slots, width), 1)).astype(F32).astype(BF16)
    pieces = split3(slab_ref[...])
    out_ref[...] = sum(dot(take, p, 1, 1, None) for p in pieces[::-1])


def pack(table, slab):
    (rows, width), step = slab.shape, 512
    return pl.pallas_call(
        pack_kernel,
        out_shape=jax.ShapeDtypeStruct((PAIR_CAP, rows), F32),
        grid=(rows // step,),
        in_specs=[VM, pl.BlockSpec((step, width), lambda k: (k, 0))],
        out_specs=pl.BlockSpec((PAIR_CAP, step), lambda k: (0, k)),
        cost_estimate=pl.CostEstimate(
            flops=6 * PAIR_CAP * slab.size, bytes_accessed=8 * slab.size, transcendentals=0
        ),
        name="pack",
    )(table, slab)


def leave_kernel(order_ref, table_ref, slab_ref, out_ref):
    place = lax.axis_index("col")
    slots, width = out_ref.shape[0], slab_ref.shape[1]
    owned = [(order_ref[k] * BLOCK) >> SHIFT == place for k in range(2)]

    @pl.when(jnp.logical_or(owned[0], owned[1]))
    def _():
        home, goes, ends, rank = (table_ref[k : k + 1, :] for k in (2, 4, 8, 9))
        slot = lax.broadcasted_iota(jnp.int32, (slots, home.shape[1]), 0)
        mine = (ends * PAIR_CAP + rank == slot) & (goes > 0) & ((home >> SHIFT) == place)
        at = jnp.sum(jnp.where(mine, home - place * width + 1, 0), axis=1, keepdims=True) - 1
        here = lax.broadcasted_iota(jnp.int32, (slots, width), 1)
        take = (at == here).astype(F32).astype(BF16)
        pieces = split3(slab_ref[...])
        out_ref[...] = sum(dot(take, p, 1, 1, None) for p in pieces[::-1])

    @pl.when(jnp.logical_not(jnp.logical_or(owned[0], owned[1])))
    def _():
        out_ref[...] = jnp.zeros(out_ref.shape, F32)


def leave(order, table, slab):
    (rows, width), step, slots = slab.shape, 512, NZ * PAIR_CAP
    return pl.pallas_call(
        leave_kernel,
        out_shape=jax.ShapeDtypeStruct((slots, rows), F32),
        grid=(rows // step,),
        in_specs=[
            pl.BlockSpec(memory_space=pltpu.SMEM),
            VM,
            pl.BlockSpec((step, width), lambda k: (k, 0)),
        ],
        out_specs=pl.BlockSpec((slots, step), lambda k: (0, k)),
        cost_estimate=pl.CostEstimate(
            flops=slab.size, bytes_accessed=8 * slab.size, transcendentals=0
        ),
        name="leave",
    )(order, table, slab)


def project_kernel(columns_ref, slab_ref, op_ref, *refs):
    *shards, rows_ref, sums_ref, all_ref = refs
    count, total = columns_ref.shape[0], all_ref.shape[0]
    start = 0
    for shard in shards:
        all_ref[start : start + shard.shape[0], :] = shard[...]
        start += shard.shape[0]
    spread = (
        columns_ref[:, 7:8] == lax.broadcasted_iota(jnp.int32, (count, total), 1)
    ).astype(F32).astype(BF16)

    @pl.when(pl.program_id(0) == 0)
    def _():
        sums_ref[...] = jnp.zeros(sums_ref.shape, F32)

    pieces = split3(all_ref[...])
    pivot = sum(dot(spread, p, 1, 0, None) for p in pieces[::-1])
    rows_ref[...] = pivot
    three = split3(pivot)
    turned = [p.T for p in three]
    sums_ref[:, :count] += dot6(three, turned)
    sums_ref[:, count : 2 * count] += dot3(split2(op_ref[...]), turned[:2], 1, 0)
    sums_ref[:, 2 * count :] += dot3(three[:2], split2(slab_ref[...]), 1, 0)


def project(columns, slab, sketch_op, shards):
    count, (rows, width), step = columns.shape[0], slab.shape, 512
    total = sum(s.shape[0] for s in shards)
    across = lambda n: pl.BlockSpec((n, step), lambda k: (0, k))
    shape = jax.ShapeDtypeStruct
    return pl.pallas_call(
        project_kernel,
        out_shape=(
            shape((count, rows), F32),
            shape((count, 2 * count + width), F32),
        ),
        grid=(rows // step,),
        in_specs=[
            VM,
            pl.BlockSpec((step, width), lambda k: (k, 0)),
            across(sketch_op.shape[0]),
            *(across(s.shape[0]) for s in shards),
        ],
        out_specs=(
            across(count),
            pl.BlockSpec((count, 2 * count + width), lambda k: (0, 0)),
        ),
        scratch_shapes=[pltpu.VMEM((total, step), F32)],
        cost_estimate=pl.CostEstimate(
            flops=6 * count * rows * (total + 2 * count + width),
            bytes_accessed=4 * (slab.size + sketch_op.size + total * rows + count * rows),
            transcendentals=0,
        ),
        name="project",
    )(columns, slab, sketch_op, *shards)


def one_hot_dot(a, b):
    return sum(dot(p, b.astype(F32).astype(BF16), 1, 0, None) for p in split3(a)[::-1])


def weigh_kernel(order_ref, columns_ref, gram_ref, inv_ref, rest_ref, sketch_ref, *outs):
    factors_ref, mix_ref, new_ref, keep_ref, sketch_out_ref = outs
    place = lax.axis_index("col")
    count, width = gram_ref.shape[0], sketch_ref.shape[1]
    pw = BLOCK
    cols = place * width + lax.broadcasted_iota(jnp.int32, (1, width), 1)
    home, goal, goes, dest_rank, met, ends_rank = (
        columns_ref[:, k : k + 1] for k in (2, 3, 4, 5, 6, 9)
    )

    def any_row(mask):
        return jnp.max(mask.astype(jnp.int32), axis=0, keepdims=True) > 0

    def spot(mask, rank, cap):
        slot = jnp.sum(jnp.where(mask, rank + 1, 0), axis=0, keepdims=True) - 1
        return lax.broadcasted_iota(jnp.int32, (cap, width), 0) == slot

    at = (goal == cols) & (goes > 0)
    is_new, is_new0 = any_row(at), any_row(at[:pw])
    put_new, put_new0 = spot(at, dest_rank, DEST_CAP), spot(at[:pw], dest_rank[:pw], DEST_CAP)
    put = home == cols
    again = ((goal == cols) & (met > 0))[pw:]
    put0 = jnp.concatenate([put[:pw].astype(F32), again.astype(F32)], axis=0)
    put = put.astype(F32)
    in0, in1 = cols >> 7 == order_ref[0], cols >> 7 == order_ref[1]
    is_old0 = jnp.logical_not(is_new0 | in0 | any_row(again))
    is_old = jnp.logical_not(is_new | in0 | in1)
    gram = gram_ref[...]
    pivot_sketch, product = rest_ref[:, :count], rest_ref[:, count : count + width]
    late = rest_ref[:, count + width :]
    new_product, new_sketch = late[:, :DEST_CAP], late[:, DEST_CAP:]
    before = jnp.where(is_old0, product, 0.0) + one_hot_dot(gram, put0)
    before += one_hot_dot(new_product, put_new0)
    after = jnp.where(is_old, product, 0.0) + one_hot_dot(gram, put)
    after += one_hot_dot(new_product, put_new)
    inverse = inv_ref[...]
    factors_ref[:pw, :] = dot(inverse[:pw], before, 1, 0)
    solved = dot(inverse, after, 1, 0)
    factors_ref[pw:, :] = jnp.where(in0, 0.0, solved[pw:])
    weights = jnp.concatenate(
        [jnp.where(in0, 0.0, solved[:pw]), jnp.where(in0 | in1, 0.0, solved[pw:])], axis=0
    )
    mix = put - dot(inverse, weights, 0, 0)
    mix_ref[...] = mix
    new_ref[...] = spot(at, ends_rank, new_ref.shape[0]).astype(F32)
    keep_ref[...] = is_old.astype(F32)
    sketch = jnp.where(is_old, sketch_ref[...], 0.0) + one_hot_dot(new_sketch, put_new)
    sketch += dot3(split2(pivot_sketch), split2(mix), 1, 0)
    sketch_out_ref[...] = jnp.where(in0 | in1, 0.0, sketch)


def weigh(order, columns, gram, inverse, rest, sketch):
    count, width = gram.shape[0], sketch.shape[1]
    shape = lambda n: jax.ShapeDtypeStruct((n, width), F32)
    return pl.pallas_call(
        weigh_kernel,
        out_shape=(shape(count), shape(count), shape(64), shape(1), shape(count)),
        in_specs=[pl.BlockSpec(memory_space=pltpu.SMEM)] + [VM] * 5,
        out_specs=(VM,) * 5,
        cost_estimate=pl.CostEstimate(
            flops=60 * count * count * width, bytes_accessed=20 * count * width, transcendentals=0
        ),
        name="weigh",
    )(order, columns, gram, inverse, rest, sketch)


def finish_kernel(slab_ref, rows_ref, own_ref, other_ref, mix_ref, new_ref, keep_ref, out_ref):
    arrived = own_ref[...] + other_ref[...]
    blank = jnp.zeros((new_ref.shape[0] - arrived.shape[0], arrived.shape[1]), F32)
    arrived = jnp.concatenate([arrived, blank], axis=0)
    pieces = split3(arrived)[::-1]
    put = new_ref[...].astype(BF16)
    total = dot3(split2(rows_ref[...]), split2(mix_ref[...]), 0, 0)
    total += sum(dot(p, put, 0, 0, None) for p in pieces)
    out_ref[...] = jnp.where(keep_ref[...] > 0.0, slab_ref[...], 0.0) + total


def finish(slab, pivot_rows, own, other, mix, new, keep):
    (rows, width), step = slab.shape, 512
    across = lambda n: pl.BlockSpec((n, step), lambda k: (0, k))
    block = pl.BlockSpec((step, width), lambda k: (k, 0))
    return pl.pallas_call(
        finish_kernel,
        out_shape=jax.ShapeDtypeStruct(slab.shape, F32),
        grid=(rows // step,),
        in_specs=[
            block,
            across(pivot_rows.shape[0]),
            across(own.shape[0]),
            across(other.shape[0]),
            VM,
            VM,
            VM,
        ],
        out_specs=block,
        cost_estimate=pl.CostEstimate(
            flops=6 * pivot_rows.size * width, bytes_accessed=8 * slab.size, transcendentals=0
        ),
        name="finish",
    )(slab, pivot_rows, own, other, mix, new, keep)


def sketch_kernel(op_ref, slab_ref, out_ref):
    @pl.when(pl.program_id(0) == 0)
    def _():
        out_ref[...] = jnp.zeros(out_ref.shape, F32)

    out_ref[...] += dot3(split2(op_ref[...]), split2(slab_ref[...]), 1, 0)


def sketch_sum(sketch_op, slab):
    count, (rows, width), step = sketch_op.shape[0], slab.shape, 512
    return pl.pallas_call(
        sketch_kernel,
        out_shape=jax.ShapeDtypeStruct((count, width), F32),
        grid=(rows // step,),
        in_specs=[
            pl.BlockSpec((count, step), lambda k: (0, k)),
            pl.BlockSpec((step, width), lambda k: (k, 0)),
        ],
        out_specs=pl.BlockSpec((count, width), lambda k: (0, 0)),
        cost_estimate=pl.CostEstimate(
            flops=6 * count * slab.size,
            bytes_accessed=4 * (slab.size + sketch_op.size),
            transcendentals=0,
        ),
        name="sketch_sum",
    )(sketch_op, slab)


def row_perm(f):
    out = []
    for x in range(NX):
        for y in range(NY):
            for c in range(NCORE):
                u, v, w = f(x, y, c)
                out.append(((x * NY + y) * NCORE + c, (u * NY + v % NY) * NCORE + w))
    return out


def col_perm(f):
    out = []
    for x in range(NXH):
        for z in range(NZ):
            u, v = f(x, z)
            out.append((x * NZ + z, u * NZ + v % NZ))
    return out


Y_UP = row_perm(lambda x, y, c: (x, y + 1, c))
Y_DOWN = row_perm(lambda x, y, c: (x, y - 1, c))
X_SWAP = row_perm(lambda x, y, c: (1 - x, y, c))
CORE_SWAP = row_perm(lambda x, y, c: (x, y, 1 - c))
Z_UP = col_perm(lambda x, z: (x, z + 1))
Z_DOWN = col_perm(lambda x, z: (x, z - 1))
XH_SWAP = col_perm(lambda x, z: (1 - x, z))


def row(x, perm):
    return lax.ppermute(x, "row", perm)


def col(x, perm):
    return lax.ppermute(x, "col", perm)


def hold_kernel(in_ref, out_ref):
    out_ref[...] = in_ref[...]


def hold(x):
    block = pl.BlockSpec((128, 512), lambda i, j: (i, j))
    return pl.pallas_call(
        hold_kernel,
        out_shape=jax.ShapeDtypeStruct(x.shape, x.dtype),
        grid=(x.shape[0] // 128, x.shape[1] // 512),
        in_specs=[block],
        out_specs=block,
        name="hold",
    )(x)


def exchange_sum(x, axis):
    n = lax.axis_size(axis)
    parts = x.reshape(n, x.shape[0] // n, *x.shape[1:])
    return jnp.sum(lax.all_to_all(parts, axis, 0, 0), axis=0)


def all_sum(x, axis):
    n = lax.axis_size(axis)
    turn = [(i, (i + 1) % n) for i in range(n)]

    def step(_, carry):
        moving, total = carry
        moving = lax.ppermute(moving, axis, turn)
        return moving, total + moving

    return lax.fori_loop(0, n - 1, step, (x, x))[1]


def spread_rows(x):
    n = lax.axis_size("row")
    copies = jnp.broadcast_to(x[None], (n, *x.shape))
    return lax.all_to_all(copies, "row", 0, 0).reshape(n * x.shape[0], x.shape[1])


def general(slab, sketch_op, block_order, pivots):
    width, pw = slab.shape[1], pivots.shape[1]
    place = lax.axis_index("col")
    base = place * width
    cols = base + jnp.arange(width, dtype=jnp.int32)
    sketch = all_sum(dot(sketch_op, slab, 1, 0, lax.Precision.HIGH), "row")

    def panel(k, carry):
        slab, sketch, finished, factors = carry
        start = block_order[k] * pw
        owner = start // width
        offset = start - owner * width
        owns = place == owner
        local = pivots[k] - base
        selector = (jnp.arange(width)[:, None] == local[None, :]).astype(F32)
        targeted = jnp.sum(selector, axis=1) > 0.5
        both = jnp.concatenate([slab, sketch])
        block = lax.dynamic_slice_in_dim(both, offset, pw, 1)
        moved = jnp.concatenate(
            [dot(both, selector, 1, 0), jnp.where(owns, block, 0.0)], axis=1
        )
        moved = all_sum(moved, "col")
        panel_cols, displaced = moved[:, :pw], moved[:, pw:]
        both = lax.dynamic_update_slice_in_dim(
            both, jnp.where(owns, panel_cols, block), offset, 1
        )
        both = jnp.where(targeted[None, :], dot(displaced, selector, 1, 1), both)
        slab, sketch = both[: slab.shape[0]], both[slab.shape[0] :]
        panel_slab, panel_sketch = panel_cols[: slab.shape[0]], panel_cols[slab.shape[0] :]
        gram = all_sum(dot(panel_slab, panel_slab, 0, 0), "row")
        inverse = inverse_factor(gram)
        basis = dot(panel_slab, inverse, 1, 1)
        projected = all_sum(dot(basis, slab, 0, 0, lax.Precision.HIGH), "row")
        factors = lax.dynamic_update_slice_in_dim(
            factors, jnp.where(finished[None, :], 0.0, projected), k * pw, 0
        )
        finished = finished | (cols // pw == block_order[k])
        slab = jnp.where(finished[None, :], slab, slab - dot(basis, projected, 1, 0, lax.Precision.HIGH))
        update = dot(dot(panel_sketch, inverse, 1, 1), projected, 1, 0, lax.Precision.HIGH)
        sketch = jnp.where(finished[None, :], 0.0, sketch - update)
        return slab, sketch, finished, factors

    carry = (
        slab,
        sketch,
        jnp.zeros((width,), dtype=bool),
        jnp.zeros((pivots.shape[0] * pw, width), F32),
    )
    slab, sketch, _, factors = lax.fori_loop(0, pivots.shape[0], panel, carry)
    return slab, factors, sketch


def joint(slab, sketch_op, block_order, pivots, table, columns):
    rows, width = slab.shape
    pw = pivots.shape[1]
    np_ = 2 * pw
    ncol = NXH * NZ
    place = lax.axis_index("col")
    z = place % NZ
    cols = place * width + jnp.arange(width, dtype=jnp.int32)
    home, goal, goes, dest_rank = table[2], table[3], table[4] > 0, table[5]
    dest = goal // width

    packed = pack(table, slab)
    sketch_part = sketch_sum(sketch_op, slab)
    other = col(packed, XH_SWAP)
    shard = packed + other
    shard, sketch_part = lax.optimization_barrier((shard, sketch_part))
    half = PAIR_CAP // 2 // 8 * 8
    up1 = col(shard, Z_UP)
    down1 = col(shard, Z_DOWN)
    leaving = leave(block_order, table, slab).reshape(NZ, PAIR_CAP, rows)
    up1, down1, leaving = lax.optimization_barrier((up1, down1, leaving))
    up2, down2 = col(up1, Z_UP), col(down1, Z_DOWN)
    sketch_part = exchange_sum(sketch_part, "row")
    up3, down3 = col(up2, Z_UP), col(down2, Z_DOWN)
    up3, down3, sketch_part = lax.optimization_barrier((up3, down3, sketch_part))
    up4, down4 = col(up3[:half], Z_UP), col(down3[half:], Z_DOWN)
    sketch = spread_rows(sketch_part)

    shards = (shard, up1, up2, up3, up4, down4, down3, down2, down1)
    pivot_rows, sums_part = project(columns, slab, sketch_op, shards)
    leaving, sums_part = lax.optimization_barrier((leaving, sums_part))
    sums = exchange_sum(sums_part, "row")

    def for_z(step):
        return lax.dynamic_index_in_dim(leaving, (z + step) % NZ, 0, keepdims=False)

    far = for_z(4)
    goes_up = col(far[:half], Z_UP)
    goes_down = col(far[half:], Z_DOWN)
    goes_up, goes_down = lax.optimization_barrier((goes_up, goes_down))

    gram, inverse = joint_factor(sums[:, :np_])
    by_goal = (
        ((dest * DEST_CAP + dest_rank)[None, :] == jnp.arange(ncol * DEST_CAP)[:, None])
        & goes[None, :]
    ).astype(F32)
    taken = (home[:, None] == cols[None, :]).astype(F32)
    pieces = jnp.concatenate([sums[:, 2 * np_ :], sketch_part], axis=0)
    small = pieces.shape[0] // 2
    sent = dot(by_goal, dot(taken, pieces, 1, 1), 1, 0)
    sent = sent.reshape(ncol, DEST_CAP, pieces.shape[0])
    sent = lax.all_to_all(sent, "col", 0, 0)
    new_sums = jnp.sum(sent, axis=0).T
    rest = jnp.concatenate([sums[:, np_:], new_sums[:small], new_sums[small:]], axis=1)
    rest = spread_rows(rest)

    goes_up = for_z(3) + jnp.pad(goes_up, ((0, PAIR_CAP - half), (0, 0)))
    goes_down = for_z(-3) + jnp.pad(goes_down, ((half, 0), (0, 0)))
    for step in (2, 1, 0):
        goes_up = col(goes_up, Z_UP)
        goes_down = col(goes_down, Z_DOWN)
        goes_up, goes_down = lax.optimization_barrier((goes_up, goes_down))
        if step > 0:
            goes_up, goes_down = for_z(step) + goes_up, for_z(-step) + goes_down
    arrived = for_z(0) + goes_up + goes_down
    other = col(arrived, XH_SWAP)
    factors, mix, new, keep, sketch_out = weigh(block_order, columns, gram, inverse, rest, sketch)
    return finish(slab, pivot_rows, arrived, other, mix, new, keep), factors, sketch_out


def local(slab, sketch_op, block_order, pivots):
    table, columns, fits = plan(block_order, pivots)
    outs = joint(slab, sketch_op, block_order, pivots, table, columns)

    def again(carry):
        results = general(hold(slab), hold(sketch_op), block_order, pivots)
        return (jnp.ones_like(fits[0]), *(hold(x) for x in results))

    outs = lax.while_loop(lambda carry: carry[0] == 0, again, (fits[0], *outs))
    return outs[1:]


def solution(mesh):
    return jax.shard_map(
        local,
        mesh=mesh,
        in_specs=(P("row", "col"), P(None, "row"), P(), P()),
        out_specs=(P("row", "col"), P(None, "col"), P(None, "col")),
        check_vma=False,
    )
```

```python
import jax
import jax.numpy as jnp
from jax import lax
from jax.experimental import pallas as pl
from jax.experimental.pallas import tpu as pltpu
from jax.sharding import PartitionSpec as P


HI = lax.Precision.HIGHEST
F32 = jnp.float32

NX, NY, NCORE, NXH, NZ = 2, 4, 2, 2, 8
PAIR_CAP = 56
DEST_CAP = 32


def dot(a, b, ca, cb, precision=HI):
    return lax.dot_general(
        a, b, (((ca,), (cb,)), ((), ())), precision=precision, preferred_element_type=F32
    )


BLOCK = 128
SHIFT = 9
STRIP = 16
VM = pl.BlockSpec(memory_space=pltpu.VMEM)
BF16 = jnp.bfloat16


def split2(x):
    high = x.astype(BF16)
    return high, (x - high.astype(F32)).astype(BF16)


def split3(x):
    high, rest = x.astype(BF16), None
    left = x - high.astype(F32)
    middle = left.astype(BF16)
    rest = (left - middle.astype(F32)).astype(BF16)
    return high, middle, rest


def dot3(a, b, ca, cb):
    a0, a1 = a
    b0, b1 = b
    return (
        dot(a0, b1, ca, cb, None) + dot(a1, b0, ca, cb, None)
    ) + dot(a0, b0, ca, cb, None)


def dot6(a, b):
    terms = ((0, 2), (2, 0), (1, 1), (0, 1), (1, 0), (0, 0))
    return sum(dot(a[i], b[j], 1, 0, None) for i, j in terms)


def factor_block(s_ref, w_ref, n):
    sub = lax.broadcasted_iota(jnp.int32, (STRIP, n), 0)
    lane = lax.broadcasted_iota(jnp.int32, (STRIP, n), 1)
    w_ref[...] = (
        lax.broadcasted_iota(jnp.int32, (n, n), 0) == lax.broadcasted_iota(jnp.int32, (n, n), 1)
    ).astype(F32)

    @pl.loop(0, n // STRIP)
    def _(k):
        start = pl.multiple_of(k * STRIP, STRIP)
        v = s_ref[pl.ds(start, STRIP), :]
        w = w_ref[pl.ds(start, STRIP), :]
        turned = pltpu.roll(v, lax.rem(n - start, n), 1)
        lanes = [jnp.broadcast_to(turned[:, m : m + 1], (STRIP, n)) for m in range(STRIP)]
        scale = jnp.zeros((STRIP, n), F32)
        for i in range(STRIP):
            pivot = lanes[i][i : i + 1, :]
            scale = jnp.where(sub == i, pivot, scale)
            if i == STRIP - 1:
                break
            f = jnp.where(sub > i, lanes[i] * (1.0 / pivot), 0.0)
            for m in range(i + 1, STRIP):
                lanes[m] = lanes[m] - f * lanes[m][i : i + 1, :]
            v = v - f * v[i : i + 1, :]
            w = w - f * w[i : i + 1, :]
        root = 1.0 / jnp.sqrt(scale)
        v, w = v * root, w * root
        w_ref[pl.ds(start, STRIP), :] = w
        below = jnp.where(lane >= start + STRIP, v, 0.0)
        update = dot(below, jnp.concatenate([v, w], axis=1), 0, 0)
        s_ref[...] = s_ref[...] - update[:, :n]
        w_ref[...] = w_ref[...] - update[:, n:]


def inverse_factor_kernel(gram_ref, out_ref, s_ref):
    s_ref[...] = gram_ref[...]
    factor_block(s_ref, out_ref, BLOCK)


def first_factor_kernel(near_ref, other_ref, gram_ref, inv_ref, lead_ref, rest_ref, s_ref):
    here = lax.axis_index("row")
    core = lax.rem(here, NCORE)
    y = lax.rem(here // NCORE, NY)
    x = here // (NCORE * NY)
    m, n = 16, BLOCK
    for c, ref in enumerate((near_ref, other_ref)):
        for t in range(NX):
            for i in range(NY):
                chunk = ((x ^ t) * NY + lax.rem(y + i, NY)) * NCORE + (core ^ c)
                at = (t * NY + i) * m
                gram_ref[pl.ds(pl.multiple_of(chunk * m, m), m), :] = ref[at : at + m, :]
    s_ref[...] = gram_ref[:n, :n]
    factor_block(s_ref, inv_ref, n)
    inv0 = inv_ref[...]
    cross = dot(gram_ref[n:, :n], inv0, 1, 1)
    lead_ref[...] = dot(cross, inv0, 1, 0)
    rest_ref[...] = gram_ref[n:, n:] - dot(cross, cross, 1, 1)


def second_factor_kernel(inv_ref, lead_ref, rest_ref, out_ref, s_ref, w_ref):
    n = BLOCK
    s_ref[...] = rest_ref[...]
    factor_block(s_ref, w_ref, n)
    inv1 = w_ref[...]
    out_ref[:n, :n] = inv_ref[...]
    out_ref[:n, n:] = jnp.zeros((n, n), F32)
    out_ref[n:, :n] = -dot(inv1, lead_ref[...], 1, 0)
    out_ref[n:, n:] = inv1


def joint_factor(mine):
    half = mine.shape[0] // 2
    up = row(mine, Y_UP)
    down = row(mine, Y_DOWN)
    up, down = lax.optimization_barrier((up, down))
    far_top = row(up[:half], Y_UP)
    far_low = row(down[half:], Y_DOWN)
    ring = jnp.concatenate([mine, down, far_top, far_low, up], axis=0)
    far = row(ring, X_SWAP)
    near = jnp.concatenate([ring, far], axis=0)
    other = row(near, CORE_SWAP)
    n = mine.shape[1]
    half = jax.ShapeDtypeStruct((BLOCK, BLOCK), F32)
    whole = jax.ShapeDtypeStruct((n, n), F32)
    cost = pl.CostEstimate(
        flops=5_000_000_000, bytes_accessed=3 * n * n * 4, transcendentals=0
    )
    scratch = pltpu.VMEM((BLOCK, BLOCK), F32)
    gram, *parts = pl.pallas_call(
        first_factor_kernel,
        out_shape=(whole, half, half, half),
        in_specs=[VM, VM],
        out_specs=(VM,) * 4,
        scratch_shapes=[scratch],
        cost_estimate=cost,
        name="joint_factor",
    )(near, other)
    inverse = pl.pallas_call(
        second_factor_kernel,
        out_shape=whole,
        in_specs=[VM] * 3,
        out_specs=VM,
        scratch_shapes=[scratch] * 2,
        cost_estimate=cost,
        name="second_factor",
    )(*parts)
    return gram, inverse


def inverse_factor(gram):
    n = gram.shape[0]
    return pl.pallas_call(
        inverse_factor_kernel,
        out_shape=jax.ShapeDtypeStruct((n, n), F32),
        in_specs=[VM],
        out_specs=VM,
        scratch_shapes=[pltpu.VMEM((BLOCK, BLOCK), F32)],
        cost_estimate=pl.CostEstimate(flops=20_000_000, bytes_accessed=2 * n * n * 4, transcendentals=0),
        name="inverse_factor",
    )(gram)


def plan_kernel(order_ref, pivots_ref, table_ref, columns_ref, fits_ref):
    place = lax.axis_index("col")
    z = lax.rem(place, NZ)
    pw, wide = BLOCK, 2 * BLOCK
    pivots = pivots_ref[...]
    pivot_cols = jnp.concatenate([pivots.astype(F32), jnp.zeros((pw - 2, pw), F32)], axis=0)
    pivot_cols = pivot_cols.T.astype(jnp.int32)
    first, second = pivots[0:1, :], pivots[1:2, :]
    sub = lax.broadcasted_iota(jnp.int32, (pw, pw), 0)
    lane = lax.broadcasted_iota(jnp.int32, (1, pw), 1)
    meet = pivot_cols[:, 0:1] == second
    met_by = pivot_cols[:, 1:2] == first
    hit = jnp.sum(meet.astype(jnp.int32), axis=0, keepdims=True)
    lost = jnp.sum(met_by.astype(jnp.int32), axis=0, keepdims=True)
    start0, start1 = order_ref[0] * pw, order_ref[1] * pw
    moved = start0 + jnp.sum(jnp.where(meet, sub, 0), axis=0, keepdims=True)
    source = jnp.concatenate([first, jnp.where(hit > 0, moved, second)], axis=1)
    home = jnp.concatenate([start0 + lane, start1 + lane], axis=1)
    goal = jnp.concatenate([first, second], axis=1)
    goes = jnp.concatenate([1 - lost, jnp.ones_like(lost)], axis=1)
    met = jnp.concatenate([jnp.zeros_like(hit), hit], axis=1)
    pair = (source >> SHIFT) & (NZ - 1)
    dest = jnp.where(goes > 0, goal >> SHIFT, -1)
    ends = jnp.where(goes > 0, dest & (NZ - 1), -1)
    blank = jnp.zeros((pw - 3, wide), F32)
    groups = jnp.concatenate(
        [pair.astype(F32), dest.astype(F32), ends.astype(F32), blank], axis=0
    ).T
    groups = groups.astype(jnp.int32)
    earlier = lax.broadcasted_iota(jnp.int32, (wide, wide), 0) < lax.broadcasted_iota(
        jnp.int32, (wide, wide), 1
    )
    pair_rank = jnp.sum(
        ((groups[:, 0:1] == pair) & earlier).astype(jnp.int32), axis=0, keepdims=True
    )
    dest_rank = jnp.sum(
        ((groups[:, 1:2] == dest) & earlier).astype(jnp.int32), axis=0, keepdims=True
    )
    ends_rank = jnp.sum(
        ((groups[:, 2:3] == ends) & earlier).astype(jnp.int32), axis=0, keepdims=True
    )
    slot = ((z - pair) & (NZ - 1)) * PAIR_CAP + pair_rank
    table = jnp.concatenate(
        [source, pair_rank, home, goal, goes, dest_rank, met, slot, ends, ends_rank]
        + [jnp.zeros_like(slot)] * 6,
        axis=0,
    )
    table_ref[...] = table
    rows = jnp.concatenate([table.astype(F32), jnp.zeros((pw - 16, wide), F32)], axis=0)
    columns_ref[...] = rows.T.astype(jnp.int32)
    most = jnp.maximum(
        jnp.max(pair_rank) - PAIR_CAP, jnp.max(jnp.where(goes > 0, dest_rank, 0)) - DEST_CAP
    )
    most = jnp.maximum(most, jnp.max(jnp.where(goes > 0, ends_rank, 0)) - PAIR_CAP)
    fits_ref[0] = (most < 0).astype(jnp.int32)


def plan(block_order, pivots):
    wide = 2 * BLOCK
    smem = pl.BlockSpec(memory_space=pltpu.SMEM)
    shape = jax.ShapeDtypeStruct
    return pl.pallas_call(
        plan_kernel,
        out_shape=(
            shape((16, wide), jnp.int32),
            shape((wide, BLOCK), jnp.int32),
            shape((1,), jnp.int32),
        ),
        in_specs=[smem, VM],
        out_specs=(VM, VM, smem),
        name="plan",
    )(block_order, pivots)


def pack_kernel(table_ref, slab_ref, out_ref):
    slots, width = out_ref.shape[0], slab_ref.shape[1]
    place = lax.axis_index("col")
    source, rank = table_ref[0:1, :], table_ref[1:2, :]
    slot = lax.broadcasted_iota(jnp.int32, (slots, source.shape[1]), 0)
    mine = (rank == slot) & ((source >> SHIFT) == place)
    at = jnp.sum(jnp.where(mine, source - place * width + 1, 0), axis=1, keepdims=True) - 1
    take = (at == lax.broadcasted_iota(jnp.int32, (slots, width), 1)).astype(F32).astype(BF16)
    pieces = split3(slab_ref[...])
    out_ref[...] = sum(dot(take, p, 1, 1, None) for p in pieces[::-1])


def pack(table, slab):
    (rows, width), step = slab.shape, 1024
    return pl.pallas_call(
        pack_kernel,
        out_shape=jax.ShapeDtypeStruct((PAIR_CAP, rows), F32),
        grid=(rows // step,),
        in_specs=[VM, pl.BlockSpec((step, width), lambda k: (k, 0))],
        out_specs=pl.BlockSpec((PAIR_CAP, step), lambda k: (0, k)),
        cost_estimate=pl.CostEstimate(
            flops=6 * PAIR_CAP * slab.size, bytes_accessed=8 * slab.size, transcendentals=0
        ),
        name="pack",
    )(table, slab)


def leave_kernel(order_ref, table_ref, slab_ref, out_ref):
    place = lax.axis_index("col")
    slots, width = out_ref.shape[0], slab_ref.shape[1]
    owned = [(order_ref[k] * BLOCK) >> SHIFT == place for k in range(2)]

    @pl.when(jnp.logical_or(owned[0], owned[1]))
    def _():
        home, goes, ends, rank = (table_ref[k : k + 1, :] for k in (2, 4, 8, 9))
        slot = lax.broadcasted_iota(jnp.int32, (slots, home.shape[1]), 0)
        mine = (ends * PAIR_CAP + rank == slot) & (goes > 0) & ((home >> SHIFT) == place)
        at = jnp.sum(jnp.where(mine, home - place * width + 1, 0), axis=1, keepdims=True) - 1
        here = lax.broadcasted_iota(jnp.int32, (slots, width), 1)
        take = (at == here).astype(F32).astype(BF16)
        pieces = split3(slab_ref[...])
        out_ref[...] = sum(dot(take, p, 1, 1, None) for p in pieces[::-1])

    @pl.when(jnp.logical_not(jnp.logical_or(owned[0], owned[1])))
    def _():
        out_ref[...] = jnp.zeros(out_ref.shape, F32)


def leave(order, table, slab):
    (rows, width), step, slots = slab.shape, 512, NZ * PAIR_CAP
    return pl.pallas_call(
        leave_kernel,
        out_shape=jax.ShapeDtypeStruct((slots, rows), F32),
        grid=(rows // step,),
        in_specs=[
            pl.BlockSpec(memory_space=pltpu.SMEM),
            VM,
            pl.BlockSpec((step, width), lambda k: (k, 0)),
        ],
        out_specs=pl.BlockSpec((slots, step), lambda k: (0, k)),
        cost_estimate=pl.CostEstimate(
            flops=slab.size, bytes_accessed=8 * slab.size, transcendentals=0
        ),
        name="leave",
    )(order, table, slab)


def project_kernel(columns_ref, slab_ref, op_ref, *refs):
    *shards, rows_ref, sums_ref, all_ref = refs
    count, total = columns_ref.shape[0], all_ref.shape[0]
    start = 0
    for shard in shards:
        all_ref[start : start + shard.shape[0], :] = shard[...]
        start += shard.shape[0]
    spread = (
        columns_ref[:, 7:8] == lax.broadcasted_iota(jnp.int32, (count, total), 1)
    ).astype(F32).astype(BF16)

    @pl.when(pl.program_id(0) == 0)
    def _():
        sums_ref[...] = jnp.zeros(sums_ref.shape, F32)

    pieces = split3(all_ref[...])
    pivot = sum(dot(spread, p, 1, 0, None) for p in pieces[::-1])
    rows_ref[...] = pivot
    three = split3(pivot)
    turned = [p.T for p in three]
    sums_ref[:, :count] += dot6(three, turned)
    sums_ref[:, count : 2 * count] += dot3(split2(op_ref[...]), turned[:2], 1, 0)
    sums_ref[:, 2 * count :] += dot3(three[:2], split2(slab_ref[...]), 1, 0)


def project(columns, slab, sketch_op, shards):
    count, (rows, width), step = columns.shape[0], slab.shape, 512
    total = sum(s.shape[0] for s in shards)
    across = lambda n: pl.BlockSpec((n, step), lambda k: (0, k))
    shape = jax.ShapeDtypeStruct
    return pl.pallas_call(
        project_kernel,
        out_shape=(
            shape((count, rows), F32),
            shape((count, 2 * count + width), F32),
        ),
        grid=(rows // step,),
        in_specs=[
            VM,
            pl.BlockSpec((step, width), lambda k: (k, 0)),
            across(sketch_op.shape[0]),
            *(across(s.shape[0]) for s in shards),
        ],
        out_specs=(
            across(count),
            pl.BlockSpec((count, 2 * count + width), lambda k: (0, 0)),
        ),
        scratch_shapes=[pltpu.VMEM((total, step), F32)],
        cost_estimate=pl.CostEstimate(
            flops=6 * count * rows * (total + 2 * count + width),
            bytes_accessed=4 * (slab.size + sketch_op.size + total * rows + count * rows),
            transcendentals=0,
        ),
        name="project",
    )(columns, slab, sketch_op, *shards)


def few_kernel(table_ref, sums_ref, sketch_ref, out_ref):
    place = lax.axis_index("col")
    slots, width = out_ref.shape[0], sketch_ref.shape[1]
    home, goal, goes, rank = (table_ref[k : k + 1, :] for k in (2, 3, 4, 5))
    slot = lax.broadcasted_iota(jnp.int32, (slots, home.shape[1]), 0)
    mine = (goal >> SHIFT) * DEST_CAP + rank == slot
    mine = mine & (goes > 0) & ((home >> SHIFT) == place)
    at = jnp.sum(jnp.where(mine, home - place * width + 1, 0), axis=1, keepdims=True) - 1
    here = lax.broadcasted_iota(jnp.int32, (slots, width), 1)
    take = (at == here).astype(F32).astype(BF16)
    both = jnp.concatenate([sums_ref[:, sums_ref.shape[1] - width :], sketch_ref[...]], axis=0)
    out_ref[...] = sum(dot(take, p, 1, 1, None) for p in split3(both)[::-1])


def few(table, sums, sketch_part):
    slots, n = NXH * NZ * DEST_CAP, 2 * sums.shape[0]
    return pl.pallas_call(
        few_kernel,
        out_shape=jax.ShapeDtypeStruct((slots, n), F32),
        in_specs=[VM] * 3,
        out_specs=VM,
        cost_estimate=pl.CostEstimate(
            flops=6 * slots * n * sketch_part.shape[1],
            bytes_accessed=8 * sums.size,
            transcendentals=0,
        ),
        name="few",
    )(table, sums, sketch_part)


def one_hot_dot(a, b):
    return sum(dot(p, b.astype(F32).astype(BF16), 1, 0, None) for p in split3(a)[::-1])


def weigh_kernel(order_ref, columns_ref, gram_ref, inv_ref, rest_ref, sketch_ref, *outs):
    factors_ref, mix_ref, new_ref, keep_ref, sketch_out_ref = outs
    place = lax.axis_index("col")
    count, width = gram_ref.shape[0], sketch_ref.shape[1]
    pw = BLOCK
    cols = place * width + lax.broadcasted_iota(jnp.int32, (1, width), 1)
    home, goal, goes, dest_rank, met, ends_rank = (
        columns_ref[:, k : k + 1] for k in (2, 3, 4, 5, 6, 9)
    )

    def any_row(mask):
        return jnp.max(mask.astype(jnp.int32), axis=0, keepdims=True) > 0

    def spot(mask, rank, cap):
        slot = jnp.sum(jnp.where(mask, rank + 1, 0), axis=0, keepdims=True) - 1
        return lax.broadcasted_iota(jnp.int32, (cap, width), 0) == slot

    at = (goal == cols) & (goes > 0)
    is_new, is_new0 = any_row(at), any_row(at[:pw])
    put_new, put_new0 = spot(at, dest_rank, DEST_CAP), spot(at[:pw], dest_rank[:pw], DEST_CAP)
    put = home == cols
    again = ((goal == cols) & (met > 0))[pw:]
    put0 = jnp.concatenate([put[:pw].astype(F32), again.astype(F32)], axis=0)
    put = put.astype(F32)
    in0, in1 = cols >> 7 == order_ref[0], cols >> 7 == order_ref[1]
    is_old0 = jnp.logical_not(is_new0 | in0 | any_row(again))
    is_old = jnp.logical_not(is_new | in0 | in1)
    gram = gram_ref[...]
    pivot_sketch, product = rest_ref[:, :count], rest_ref[:, count : count + width]
    late = rest_ref[:, count + width :]
    new_product, new_sketch = late[:, :DEST_CAP], late[:, DEST_CAP:]
    before = jnp.where(is_old0, product, 0.0) + one_hot_dot(gram, put0)
    before += one_hot_dot(new_product, put_new0)
    after = jnp.where(is_old, product, 0.0) + one_hot_dot(gram, put)
    after += one_hot_dot(new_product, put_new)
    inverse = inv_ref[...]
    factors_ref[:pw, :] = dot(inverse[:pw], before, 1, 0)
    solved = dot(inverse, after, 1, 0)
    factors_ref[pw:, :] = jnp.where(in0, 0.0, solved[pw:])
    weights = jnp.concatenate(
        [jnp.where(in0, 0.0, solved[:pw]), jnp.where(in0 | in1, 0.0, solved[pw:])], axis=0
    )
    mix = put - dot(inverse, weights, 0, 0)
    mix_ref[...] = mix
    new_ref[...] = spot(at, ends_rank, new_ref.shape[0]).astype(F32)
    keep_ref[...] = is_old.astype(F32)
    sketch = jnp.where(is_old, sketch_ref[...], 0.0) + one_hot_dot(new_sketch, put_new)
    sketch += dot3(split2(pivot_sketch), split2(mix), 1, 0)
    sketch_out_ref[...] = jnp.where(in0 | in1, 0.0, sketch)


def weigh(order, columns, gram, inverse, rest, sketch):
    count, width = gram.shape[0], sketch.shape[1]
    shape = lambda n: jax.ShapeDtypeStruct((n, width), F32)
    return pl.pallas_call(
        weigh_kernel,
        out_shape=(shape(count), shape(count), shape(64), shape(1), shape(count)),
        in_specs=[pl.BlockSpec(memory_space=pltpu.SMEM)] + [VM] * 5,
        out_specs=(VM,) * 5,
        cost_estimate=pl.CostEstimate(
            flops=60 * count * count * width, bytes_accessed=20 * count * width, transcendentals=0
        ),
        name="weigh",
    )(order, columns, gram, inverse, rest, sketch)


def finish_kernel(slab_ref, rows_ref, own_ref, other_ref, mix_ref, new_ref, keep_ref, out_ref):
    arrived = own_ref[...] + other_ref[...]
    blank = jnp.zeros((new_ref.shape[0] - arrived.shape[0], arrived.shape[1]), F32)
    arrived = jnp.concatenate([arrived, blank], axis=0)
    pieces = split3(arrived)[::-1]
    put = new_ref[...].astype(BF16)
    total = dot3(split2(rows_ref[...]), split2(mix_ref[...]), 0, 0)
    total += sum(dot(p, put, 0, 0, None) for p in pieces)
    out_ref[...] = jnp.where(keep_ref[...] > 0.0, slab_ref[...], 0.0) + total


def finish(slab, pivot_rows, own, other, mix, new, keep):
    (rows, width), step = slab.shape, 1024
    across = lambda n: pl.BlockSpec((n, step), lambda k: (0, k))
    block = pl.BlockSpec((step, width), lambda k: (k, 0))
    return pl.pallas_call(
        finish_kernel,
        out_shape=jax.ShapeDtypeStruct(slab.shape, F32),
        grid=(rows // step,),
        in_specs=[
            block,
            across(pivot_rows.shape[0]),
            across(own.shape[0]),
            across(other.shape[0]),
            VM,
            VM,
            VM,
        ],
        out_specs=block,
        cost_estimate=pl.CostEstimate(
            flops=6 * pivot_rows.size * width, bytes_accessed=8 * slab.size, transcendentals=0
        ),
        name="finish",
    )(slab, pivot_rows, own, other, mix, new, keep)


def sketch_kernel(op_ref, slab_ref, out_ref):
    @pl.when(pl.program_id(0) == 0)
    def _():
        out_ref[...] = jnp.zeros(out_ref.shape, F32)

    out_ref[...] += dot3(split2(op_ref[...]), split2(slab_ref[...]), 1, 0)


def sketch_sum(sketch_op, slab):
    count, (rows, width), step = sketch_op.shape[0], slab.shape, 512
    return pl.pallas_call(
        sketch_kernel,
        out_shape=jax.ShapeDtypeStruct((count, width), F32),
        grid=(rows // step,),
        in_specs=[
            pl.BlockSpec((count, step), lambda k: (0, k)),
            pl.BlockSpec((step, width), lambda k: (k, 0)),
        ],
        out_specs=pl.BlockSpec((count, width), lambda k: (0, 0)),
        cost_estimate=pl.CostEstimate(
            flops=6 * count * slab.size,
            bytes_accessed=4 * (slab.size + sketch_op.size),
            transcendentals=0,
        ),
        name="sketch_sum",
    )(sketch_op, slab)


def row_perm(f):
    out = []
    for x in range(NX):
        for y in range(NY):
            for c in range(NCORE):
                u, v, w = f(x, y, c)
                out.append(((x * NY + y) * NCORE + c, (u * NY + v % NY) * NCORE + w))
    return out


def col_perm(f):
    out = []
    for x in range(NXH):
        for z in range(NZ):
            u, v = f(x, z)
            out.append((x * NZ + z, u * NZ + v % NZ))
    return out


Y_UP = row_perm(lambda x, y, c: (x, y + 1, c))
Y_DOWN = row_perm(lambda x, y, c: (x, y - 1, c))
X_SWAP = row_perm(lambda x, y, c: (1 - x, y, c))
CORE_SWAP = row_perm(lambda x, y, c: (x, y, 1 - c))
Z_UP = col_perm(lambda x, z: (x, z + 1))
Z_DOWN = col_perm(lambda x, z: (x, z - 1))
XH_SWAP = col_perm(lambda x, z: (1 - x, z))


def row(x, perm):
    return lax.ppermute(x, "row", perm)


def col(x, perm):
    return lax.ppermute(x, "col", perm)


def hold_kernel(in_ref, out_ref):
    out_ref[...] = in_ref[...]


def hold(x):
    block = pl.BlockSpec((128, 512), lambda i, j: (i, j))
    return pl.pallas_call(
        hold_kernel,
        out_shape=jax.ShapeDtypeStruct(x.shape, x.dtype),
        grid=(x.shape[0] // 128, x.shape[1] // 512),
        in_specs=[block],
        out_specs=block,
        name="hold",
    )(x)


def exchange_sum(x, axis):
    n = lax.axis_size(axis)
    parts = x.reshape(n, x.shape[0] // n, *x.shape[1:])
    return jnp.sum(lax.all_to_all(parts, axis, 0, 0), axis=0)


def all_sum(x, axis):
    n = lax.axis_size(axis)
    turn = [(i, (i + 1) % n) for i in range(n)]

    def step(_, carry):
        moving, total = carry
        moving = lax.ppermute(moving, axis, turn)
        return moving, total + moving

    return lax.fori_loop(0, n - 1, step, (x, x))[1]


def spread_rows(x):
    n = lax.axis_size("row")
    copies = jnp.broadcast_to(x[None], (n, *x.shape))
    return lax.all_to_all(copies, "row", 0, 0).reshape(n * x.shape[0], x.shape[1])


def general(slab, sketch_op, block_order, pivots):
    width, pw = slab.shape[1], pivots.shape[1]
    place = lax.axis_index("col")
    base = place * width
    cols = base + jnp.arange(width, dtype=jnp.int32)
    sketch = all_sum(dot(sketch_op, slab, 1, 0, lax.Precision.HIGH), "row")

    def panel(k, carry):
        slab, sketch, finished, factors = carry
        start = block_order[k] * pw
        owner = start // width
        offset = start - owner * width
        owns = place == owner
        local = pivots[k] - base
        selector = (jnp.arange(width)[:, None] == local[None, :]).astype(F32)
        targeted = jnp.sum(selector, axis=1) > 0.5
        both = jnp.concatenate([slab, sketch])
        block = lax.dynamic_slice_in_dim(both, offset, pw, 1)
        moved = jnp.concatenate(
            [dot(both, selector, 1, 0), jnp.where(owns, block, 0.0)], axis=1
        )
        moved = all_sum(moved, "col")
        panel_cols, displaced = moved[:, :pw], moved[:, pw:]
        both = lax.dynamic_update_slice_in_dim(
            both, jnp.where(owns, panel_cols, block), offset, 1
        )
        both = jnp.where(targeted[None, :], dot(displaced, selector, 1, 1), both)
        slab, sketch = both[: slab.shape[0]], both[slab.shape[0] :]
        panel_slab, panel_sketch = panel_cols[: slab.shape[0]], panel_cols[slab.shape[0] :]
        gram = all_sum(dot(panel_slab, panel_slab, 0, 0), "row")
        inverse = inverse_factor(gram)
        basis = dot(panel_slab, inverse, 1, 1)
        projected = all_sum(dot(basis, slab, 0, 0, lax.Precision.HIGH), "row")
        factors = lax.dynamic_update_slice_in_dim(
            factors, jnp.where(finished[None, :], 0.0, projected), k * pw, 0
        )
        finished = finished | (cols // pw == block_order[k])
        slab = jnp.where(finished[None, :], slab, slab - dot(basis, projected, 1, 0, lax.Precision.HIGH))
        update = dot(dot(panel_sketch, inverse, 1, 1), projected, 1, 0, lax.Precision.HIGH)
        sketch = jnp.where(finished[None, :], 0.0, sketch - update)
        return slab, sketch, finished, factors

    carry = (
        slab,
        sketch,
        jnp.zeros((width,), dtype=bool),
        jnp.zeros((pivots.shape[0] * pw, width), F32),
    )
    slab, sketch, _, factors = lax.fori_loop(0, pivots.shape[0], panel, carry)
    return slab, factors, sketch


def joint(slab, sketch_op, block_order, pivots, table, columns):
    rows, _ = slab.shape
    pw = pivots.shape[1]
    np_ = 2 * pw
    ncol = NXH * NZ
    place = lax.axis_index("col")
    z = place % NZ
    packed = pack(table, slab)
    sketch_part = sketch_sum(sketch_op, slab)
    other = col(packed, XH_SWAP)
    shard = packed + other
    shard, sketch_part = lax.optimization_barrier((shard, sketch_part))
    half = PAIR_CAP // 2 // 8 * 8
    up1 = col(shard, Z_UP)
    down1 = col(shard, Z_DOWN)
    leaving = leave(block_order, table, slab).reshape(NZ, PAIR_CAP, rows)
    up1, down1 = lax.optimization_barrier((up1, down1))
    up2 = col(up1, Z_UP)
    down2 = col(down1, Z_DOWN)
    sketch_part = exchange_sum(sketch_part, "row")
    up3, down3 = col(up2, Z_UP), col(down2, Z_DOWN)
    up3, down3, sketch_part = lax.optimization_barrier((up3, down3, sketch_part))
    up4, down4 = col(up3[:half], Z_UP), col(down3[half:], Z_DOWN)
    sketch = spread_rows(sketch_part)

    shards = (shard, up1, up2, up3, up4, down4, down3, down2, down1)
    pivot_rows, sums_part = project(columns, slab, sketch_op, shards)
    leaving, sums_part = lax.optimization_barrier((leaving, sums_part))
    sums = exchange_sum(sums_part, "row")

    def for_z(step):
        return lax.dynamic_index_in_dim(leaving, (z + step) % NZ, 0, keepdims=False)

    far = for_z(4)
    goes_up = col(far[:half], Z_UP)
    goes_down = col(far[half:], Z_DOWN)
    goes_up, goes_down = lax.optimization_barrier((goes_up, goes_down))

    gram, inverse = joint_factor(sums[:, :np_])
    small = sums.shape[0]
    sent = few(table, sums, sketch_part)
    sent = sent.reshape(ncol, DEST_CAP, 2 * small)
    sent = lax.all_to_all(sent, "col", 0, 0)
    new_sums = jnp.sum(sent, axis=0).T
    rest = jnp.concatenate([sums[:, np_:], new_sums[:small], new_sums[small:]], axis=1)
    rest = spread_rows(rest)

    goes_up = for_z(3) + jnp.pad(goes_up, ((0, PAIR_CAP - half), (0, 0)))
    goes_down = for_z(-3) + jnp.pad(goes_down, ((half, 0), (0, 0)))
    for step in (2, 1, 0):
        goes_up = col(goes_up, Z_UP)
        goes_down = col(goes_down, Z_DOWN)
        goes_up, goes_down = lax.optimization_barrier((goes_up, goes_down))
        if step > 0:
            goes_up, goes_down = for_z(step) + goes_up, for_z(-step) + goes_down
    arrived = for_z(0) + goes_up + goes_down
    other = col(arrived, XH_SWAP)
    factors, mix, new, keep, sketch_out = weigh(block_order, columns, gram, inverse, rest, sketch)
    return finish(slab, pivot_rows, arrived, other, mix, new, keep), factors, sketch_out


def local(slab, sketch_op, block_order, pivots):
    table, columns, fits = plan(block_order, pivots)
    outs = joint(slab, sketch_op, block_order, pivots, table, columns)

    def again(carry):
        results = general(hold(slab), hold(sketch_op), block_order, pivots)
        return (jnp.ones_like(fits[0]), *(hold(x) for x in results))

    outs = lax.while_loop(lambda carry: carry[0] == 0, again, (fits[0], *outs))
    return outs[1:]


def solution(mesh):
    return jax.shard_map(
        local,
        mesh=mesh,
        in_specs=(P("row", "col"), P(None, "row"), P(), P()),
        out_specs=(P("row", "col"), P(None, "col"), P(None, "col")),
        check_vma=False,
    )
```
